256 devices in a mesh: seq: 32 (over y, z), head: 8 (over x, core).
Axes of the slice: x: 4, y: 4, z: 8, core: 2. Of those that a mesh axis runs over, the one named last changes fastest.
Arguments:
- tokens: bfloat16 [32768, 4096], P('seq'), may hold values from -50 to 50
- norm_gain: float32 [4096], replicated, may hold values from 0.1 to 1.9
- wq: bfloat16 [4096, 4096], P('seq', 'head'), may hold values from -2.34375 to 2.34375
- wk: bfloat16 [4096, 1024], P('seq', 'head'), may hold values from -0.09375 to 0.09375
- wv: bfloat16 [4096, 1024], P('seq', 'head'), may hold values from -0.09375 to 0.09375
- wo: bfloat16 [4096, 4096], P('head', 'seq'), may hold values from -0.1875 to 0.1875
- gate_bias: float32 [32], P('head'), may hold values from -3 to 3
- mem_init: float32 [8, 128, 128], P('head'), may hold values from -32768 to 32768
- norm_init: float32 [8, 128], P('head'), may hold values from 512 to 2048
Outputs:
- attended: bfloat16 [32768, 4096], P('seq', 'head')
The draws below stay inside these ranges and needn't reach their ends.
All inputs are finite; a program needn't handle non-finite values.
Results may differ from the reference program's by a relative error of at most 0.018.
Values may be sent and summed in bfloat16 or wider, within the bound.
No kernel may reach another device: no remote copies, remote signals or barrier semaphores. Data moves between devices by JAX's collectives and lax.ppermute only.
A program may use at most 128 MiB of HBM per device.

```python
import math
import jax
import jax.numpy as jnp
from jax import lax

D = 4096
H = 32
KVH = 8
HD = 128
SEG = 512
TOK_DEV = 1024
TOKENS = 32768
N_HEAD = 8


def shared_keys(key):
    base_draw = jax.random.normal(jax.random.fold_in(key, 11), (D, KVH * HD), jnp.float32)
    return jnp.clip(base_draw, -6.0, 6.0) / math.sqrt(D)


def draw_wk(key, part):
    return shared_keys(key).astype(jnp.bfloat16)


def draw_wq(key, part):
    noise = jax.random.normal(jax.random.fold_in(key, 12), (D, H * HD), jnp.float32)
    noise = jnp.clip(noise, -6.0, 6.0) / math.sqrt(D)
    return noise.astype(jnp.bfloat16)


def draw_tokens(key, part):
    first_key = jax.random.fold_in(key, 21)
    second_key = jax.random.fold_in(key, 22)
    offsets = jnp.clip(jax.random.normal(second_key, (TOKENS // SEG, D), jnp.float32), -3.0, 3.0)
    noise = jnp.clip(jax.random.normal(first_key, (TOKENS, D), jnp.float32), -5.0, 5.0)
    rows = noise + jnp.repeat(offsets, SEG, axis=0)
    rows = jnp.clip(rows, -50.0, 50.0)
    return rows.astype(jnp.bfloat16)


def raised(array, own_key, source, target, shards_of, factor):
    def block_of(dim):
        return (jnp.arange(array.shape[dim]) // (array.shape[dim] // shards_of)).reshape((-1,) + (1,) * (array.ndim - 1 - dim))

    near = jax.random.permutation(own_key, shards_of)[block_of(target)]
    other_side = (block_of(target) + shards_of // 2) % shards_of
    return jnp.where((block_of(source) == near) | (block_of(source) == other_side), factor * array, array)


def block_levels(key, extent, cuts, smallest, top_value):
    loudness, own = 1.0, jax.random.fold_in(key, 6)
    for position, blocks in cuts:
        heights = jnp.exp(jax.random.uniform(jax.random.fold_in(own, position), (blocks,), jnp.float32, smallest / len(cuts), top_value / len(cuts)))
        loudness = loudness * jnp.repeat(heights, extent[position] // blocks).reshape([-1 if axis == position else 1 for axis in range(len(extent))])
    return loudness


def normal_values(key, extent, spread, limit, split=(), dtype=jnp.bfloat16):
    level = block_levels(key, extent, split, -0.22, 0.18) if split else 1.0
    drawn = jax.random.normal(key, extent, jnp.float32) * spread * level
    return jnp.minimum(jnp.maximum(drawn, -limit), limit).astype(dtype)


def heavy_noise(stream_key, extent, width, most, shards, heavy, dtype=jnp.bfloat16):
    result = width * jax.random.normal(stream_key, extent, jnp.float32)
    if shards:
        result = result * block_levels(stream_key, extent, shards, -0.22, 0.18)
    return jnp.clip(raised(result, jax.random.fold_in(stream_key, 3), *heavy), -most, most).astype(dtype)


def setup_inputs(seed: int = 0) -> dict:
    splits = jax.random.split(jax.random.key(seed), 10)
    tokens = draw_tokens(jax.random.fold_in(splits[9], 71), 0)
    norm_gain = jnp.clip(1.0 + 0.18 * jax.random.normal(splits[1], (D,), jnp.float32), 0.1, 1.9)
    wq = draw_wq(jax.random.fold_in(splits[9], 71), 0)
    wk = draw_wk(jax.random.fold_in(splits[9], 71), 0)
    wv = normal_values(splits[4], (D, KVH * HD), D ** -0.5, 0.09375, ((0, 32), (1, 8)))
    wo = heavy_noise(splits[5], (H * HD, D), (H * HD) ** -0.5, 0.1875, ((0, 8), (1, 32)), (0, 1, 32, 2.75))
    gate_bias = jnp.clip(jax.random.uniform(splits[6], (H,), jnp.float32, -3.0, 3.0) * block_levels(splits[6], (H,), ((0, 8),), -0.4, 0.0), -3.0, 3.0)
    mem_init = normal_values(splits[7], (KVH, HD, HD), (6 * TOK_DEV), 32768.0, ((0, 8),), jnp.float32)
    norm_init = jnp.clip(512.0 + 1536.0 * jax.random.uniform(splits[8], (KVH, HD), jnp.float32) ** block_levels(splits[8], (KVH, HD), ((0, 8),), -0.2, 0.2), 512.0, 2048.0)
    return dict(tokens=tokens, norm_gain=norm_gain, wq=wq, wk=wk, wv=wv, wo=wo, gate_bias=gate_bias, mem_init=mem_init, norm_init=norm_init)


def feature_map(values_in):
    return jnp.where(values_in > 0, values_in + 1.0, jnp.exp(jnp.minimum(values_in, 0.0)))

def reference(tokens, norm_gain, wq, wk, wv, wo, gate_bias, mem_init, norm_init):
    highest = lax.Precision.HIGHEST
    widened = tokens.astype(jnp.float32)
    normed = (widened * lax.rsqrt(lax.optimization_barrier(jnp.mean(widened * widened, axis=-1, keepdims=True)) + 1e-05) * norm_gain).astype(jnp.bfloat16)
    queries = jnp.dot(normed, wq, preferred_element_type=jnp.float32).astype(jnp.bfloat16)
    keys_all = jnp.dot(normed, wk, preferred_element_type=jnp.float32).astype(jnp.bfloat16)
    values_all = jnp.dot(normed, wv, preferred_element_type=jnp.float32).astype(jnp.bfloat16)
    group = H // KVH
    segments = TOKENS // SEG
    query_seg = queries.reshape(segments, SEG, KVH, group, HD)
    key_seg = keys_all.reshape(segments, SEG, KVH, HD)
    value_seg = values_all.reshape(segments, SEG, KVH, HD)
    key_feats = feature_map(key_seg.astype(jnp.float32))
    delta_mem = jnp.einsum('nski,nskj->nkij', key_feats, value_seg.astype(jnp.float32), precision=highest)
    delta_norm = lax.optimization_barrier(jnp.sum(key_feats, axis=1))
    zero_mem = jnp.zeros((1, KVH, HD, HD), jnp.float32)
    zero_norm = jnp.zeros((1, KVH, HD), jnp.float32)
    mem_before = mem_init[None] + jnp.concatenate([zero_mem, jnp.cumsum(delta_mem, axis=0)[:-1]], axis=0)
    norm_before = norm_init[None] + jnp.concatenate([zero_norm, jnp.cumsum(delta_norm, axis=0)[:-1]], axis=0)
    gate_mix = jax.nn.sigmoid(gate_bias).reshape(KVH, group)
    score_scale = 1.0 / math.sqrt(HD)
    causal = lax.broadcasted_iota(jnp.int32, (SEG, SEG), 0) >= lax.broadcasted_iota(jnp.int32, (SEG, SEG), 1)

    def one_segment(operands):
        query_blk, key_blk, value_blk, memory, normer = operands
        query_feats = feature_map(query_blk.astype(jnp.float32))
        numer = jnp.einsum('skgi,kij->skgj', query_feats, memory, precision=highest)
        denom = jnp.einsum('skgi,ki->skg', query_feats, normer, precision=highest)
        retrieved = numer / denom[..., None]
        scores = jnp.einsum('qkgd,skd->kgqs', query_blk.astype(jnp.float32), key_blk.astype(jnp.float32), precision=highest) * score_scale
        scores = jnp.where(causal, scores, -1e+30)
        peak = lax.optimization_barrier(jnp.max(scores, axis=-1, keepdims=True))
        expd = jnp.exp(scores - peak)
        probs = (expd / lax.optimization_barrier(jnp.sum(expd, axis=-1, keepdims=True))).astype(jnp.bfloat16)
        local = jnp.einsum('kgqs,skd->qkgd', probs.astype(jnp.float32), value_blk.astype(jnp.float32), precision=highest)
        mixed = gate_mix[None, :, :, None] * retrieved + (1.0 - gate_mix)[None, :, :, None] * local
        return mixed.astype(jnp.bfloat16)
    mixed_all = lax.map(one_segment, (query_seg, key_seg, value_seg, mem_before, norm_before))
    mixed_all = mixed_all.reshape(TOKENS, H * HD)
    width_group = H * HD // N_HEAD
    summed = jnp.zeros((TOKENS, D), jnp.float32)
    for block in range(N_HEAD):
        partial_out = jnp.dot(mixed_all[:, block * width_group:(block + 1) * width_group], wo[block * width_group:(block + 1) * width_group], preferred_element_type=jnp.float32)
        rounded = lax.optimization_barrier(partial_out.astype(jnp.bfloat16))
        summed = summed + rounded.astype(jnp.float32)
    return summed.astype(jnp.bfloat16)
```

```python
import functools
import math

import jax
import jax.numpy as jnp
from jax import lax
from jax.experimental import pallas as pl
from jax.experimental.pallas import tpu as pltpu
from jax.sharding import PartitionSpec as P

HD = 128
SEG = 512
NY, NZ, NX = 4, 8, 4
SEQ = NY * NZ
HEADS = 2 * NX
F32 = jnp.float32
BF16 = jnp.bfloat16


def z_move(block, distance):
    return lax.ppermute(
        block, "seq", [(y * NZ + z, y * NZ + (z + distance) % NZ) for y in range(NY) for z in range(NZ)]
    )


def z_swap(block, bit):
    return lax.ppermute(block, "seq", [(s, s ^ bit) for s in range(SEQ)])


def y_move(block, distance):
    return lax.ppermute(
        block, "seq", [(y * NZ + z, (y + distance) % NY * NZ + z) for y in range(NY) for z in range(NZ)]
    )


def x_move(block, distance):
    return lax.ppermute(
        block, "head", [(2 * x + c, 2 * ((x + distance) % NX) + c) for x in range(NX) for c in range(2)]
    )


def core_swap(block):
    return lax.ppermute(block, "head", [(h, h ^ 1) for h in range(HEADS)])


def spread_wo(block):
    pairs = []
    for y in range(NY):
        for z in range(NZ):
            for h in range(HEADS):
                pairs.append(((4 * h + y) * HEADS + z, (y * NZ + z) * HEADS + h))
    return lax.ppermute(block, ("seq", "head"), pairs)


def feature_map(values_in):
    return jnp.where(values_in > 0, values_in + 1.0, jnp.exp(jnp.minimum(values_in, 0.0)))


def split(wide):
    high = wide.astype(BF16)
    return high, (wide - high.astype(F32)).astype(BF16)


def norm_kernel(order, x_ref, gain_ref, out_ref):
    wide = x_ref[...].astype(F32)
    scale = lax.rsqrt(jnp.mean(wide * wide, axis=-1, keepdims=True) + 1e-05)
    for block in range(SEQ):
        at = pl.ds(pl.multiple_of(order[block] * HD, HD), HD)
        part = x_ref[:, at].astype(F32) * scale * gain_ref[:, at]
        out_ref[:, block * HD : (block + 1) * HD] = part.astype(BF16)


def norm_call(tokens, gain, order):
    rows, width = tokens.shape
    tile = 128
    return pl.pallas_call(
        norm_kernel,
        out_shape=jax.ShapeDtypeStruct((rows, width), BF16),
        grid_spec=pltpu.PrefetchScalarGridSpec(
            num_scalar_prefetch=1,
            grid=(rows // tile,),
            in_specs=[
                pl.BlockSpec((tile, width), lambda i, o: (i, 0)),
                pl.BlockSpec((1, width), lambda i, o: (0, 0)),
            ],
            out_specs=pl.BlockSpec((tile, width), lambda i, o: (i, 0)),
        ),
        cost_estimate=pl.CostEstimate(flops=6 * rows * width, bytes_accessed=4 * rows * width, transcendentals=rows),
        name="norm",
    )(order, tokens, gain.reshape(1, width))


def qkv_kernel(x_ref, *refs):
    wq_refs, wkv_refs = refs[:9], refs[9:13]
    q_ref, k_ref, v_ref, delta_ref = refs[13:]
    wide = None
    at = 0
    for w_ref in wq_refs:
        depth = w_ref.shape[0] * HD
        term = jnp.dot(
            x_ref[:, at : at + depth], w_ref[...].reshape(depth, 4 * HD), preferred_element_type=F32
        )
        wide = term if wide is None else wide + term
        at += depth
    q_ref[...] = wide.astype(BF16)
    wide = None
    for e, w_ref in enumerate(wkv_refs):
        columns = jnp.concatenate(
            [x_ref[:, (4 * o + e) * HD : (4 * o + e + 1) * HD] for o in range(NZ)], axis=1
        )
        term = jnp.dot(columns, w_ref[...].reshape(NZ * HD, 2 * HD), preferred_element_type=F32)
        wide = term if wide is None else wide + term
    keys = wide[:, :HD].astype(BF16)
    values = wide[:, HD:].astype(BF16)
    k_ref[...] = keys
    v_ref[...] = values
    feats = feature_map(keys.astype(F32))
    high, low = split(feats)
    by_rows = (((0,), (0,)), ((), ()))
    memory = lax.dot_general(high, values, by_rows, preferred_element_type=F32)
    memory += lax.dot_general(low, values, by_rows, preferred_element_type=F32)
    delta_ref[0, :HD, :] = memory
    delta_ref[0, HD:, :] = jnp.broadcast_to(jnp.sum(feats, axis=0, keepdims=True), (8, HD))


def whole(array, steps=1):
    return pl.BlockSpec(array.shape, lambda i, n=array.ndim: (0,) * n, pipeline_mode=pl.Buffered(1))


def qkv_call(normed, wq_pieces, wkv_pieces):
    rows, width = normed.shape
    segments = rows // SEG
    row_block = lambda n: pl.BlockSpec((SEG, n), lambda i: (i, 0))
    pieces = [*wq_pieces, *wkv_pieces]
    return pl.pallas_call(
        qkv_kernel,
        grid=(segments,),
        out_shape=[
            jax.ShapeDtypeStruct((rows, 4 * HD), BF16),
            jax.ShapeDtypeStruct((rows, HD), BF16),
            jax.ShapeDtypeStruct((rows, HD), BF16),
            jax.ShapeDtypeStruct((segments, HD + 8, HD), F32),
        ],
        in_specs=[row_block(width), *[whole(p) for p in pieces]],
        out_specs=[
            row_block(4 * HD),
            row_block(HD),
            row_block(HD),
            pl.BlockSpec((1, HD + 8, HD), lambda i: (i, 0, 0)),
        ],
        cost_estimate=pl.CostEstimate(flops=2 * rows * width * 6 * HD, bytes_accessed=16 << 20, transcendentals=rows * HD),
        compiler_params=pltpu.CompilerParams(vmem_limit_bytes=40 << 20),
        name="qkv",
    )(normed, *pieces)


def local_kernel(q_ref, k_ref, v_ref, out_ref):
    scale = 1.0 / math.sqrt(HD)
    half = SEG // 2
    transposed = (((1,), (1,)), ((), ()))
    for head in range(4):
        for part in range(2):
            rows = slice(part * half, (part + 1) * half)
            seen = (part + 1) * half
            query = q_ref[rows, head * HD : (head + 1) * HD]
            scores = lax.dot_general(query, k_ref[:seen, :], transposed, preferred_element_type=F32) * scale
            row = lax.broadcasted_iota(jnp.int32, (half, seen), 0) + part * half
            column = lax.broadcasted_iota(jnp.int32, (half, seen), 1)
            scores = jnp.where(row >= column, scores, -1e30)
            expd = jnp.exp(scores - jnp.max(scores, axis=-1, keepdims=True))
            probs = (expd / jnp.sum(expd, axis=-1, keepdims=True)).astype(BF16)
            out_ref[rows, head * HD : (head + 1) * HD] = jnp.dot(
                probs, v_ref[:seen, :], preferred_element_type=F32
            )


def local_call(queries, keys, values):
    rows = queries.shape[0]
    row_block = lambda n: pl.BlockSpec((SEG, n), lambda i: (i, 0))
    return pl.pallas_call(
        local_kernel,
        grid=(rows // SEG,),
        out_shape=jax.ShapeDtypeStruct((rows, 4 * HD), F32),
        in_specs=[row_block(4 * HD), row_block(HD), row_block(HD)],
        out_specs=row_block(4 * HD),
        cost_estimate=pl.CostEstimate(flops=16 * rows * SEG * HD, bytes_accessed=4 << 20, transcendentals=4 * rows * SEG),
        compiler_params=pltpu.CompilerParams(vmem_limit_bytes=24 << 20),
        name="local",
    )(queries, keys, values)


def mix_kernel(gate_ref, q_ref, local_ref, memory_ref, out_ref):
    memory = memory_ref[:HD, :]
    normer = jnp.broadcast_to(memory_ref[HD : HD + 1, :], (HD, HD)).T
    both_high, both_low = split(jnp.concatenate([memory, normer], axis=1))
    for head in range(4):
        at = slice(head * HD, (head + 1) * HD)
        high, low = split(feature_map(q_ref[:, at].astype(F32)))
        both = jnp.dot(high, both_high, preferred_element_type=F32)
        both += jnp.dot(high, both_low, preferred_element_type=F32)
        both += jnp.dot(low, both_high, preferred_element_type=F32)
        gate = gate_ref[head]
        mixed = gate * (both[:, :HD] / both[:, HD:]) + (1.0 - gate) * local_ref[:, at]
        out_ref[:, at] = mixed.astype(BF16)


def mix_call(gate, queries, local, memory, segment):
    row_block = pl.BlockSpec((SEG, 4 * HD), lambda i: (segment, 0))
    return pl.pallas_call(
        mix_kernel,
        grid=(1,),
        out_shape=jax.ShapeDtypeStruct((SEG, 4 * HD), BF16),
        in_specs=[
            pl.BlockSpec(memory_space=pltpu.SMEM),
            row_block,
            row_block,
            pl.BlockSpec((HD + 8, HD), lambda i: (0, 0)),
        ],
        out_specs=pl.BlockSpec((SEG, 4 * HD), lambda i: (0, 0)),
        cost_estimate=pl.CostEstimate(flops=48 * SEG * HD * HD, bytes_accessed=2 << 20, transcendentals=4 * SEG * HD),
        compiler_params=pltpu.CompilerParams(vmem_limit_bytes=16 << 20),
        name="mix",
    )(gate, queries, local, memory)


def out_kernel(count, last, order, *refs):
    mixed_refs, w_ref = refs[: 2 * count], refs[2 * count]
    out_ref = refs[-1]
    totals = [refs[2 * count + 1][s * SEG : (s + 1) * SEG, :] if last else None for s in range(2)]
    for p in range(count):
        rows = order[p]
        weight = jnp.concatenate([w_ref[j, rows] for j in range(4)], axis=1)
        for s in range(2):
            term = jnp.dot(mixed_refs[2 * p + s][...], weight, preferred_element_type=F32)
            totals[s] = term if totals[s] is None else totals[s] + term
    for s in range(2):
        out_ref[s * SEG : (s + 1) * SEG, :] = totals[s].astype(out_ref.dtype)


def out_call(order, pieces, weight, so_far=None):
    count = len(pieces)
    flat = [part for piece in pieces for part in piece]
    last = so_far is not None
    extra = [so_far] if last else []
    vmem = pl.BlockSpec(memory_space=pltpu.VMEM)
    return pl.pallas_call(
        functools.partial(out_kernel, count, last),
        out_shape=jax.ShapeDtypeStruct((2 * SEG, 4 * HD), BF16 if last else F32),
        in_specs=[pl.BlockSpec(memory_space=pltpu.SMEM)] + [vmem] * (len(flat) + 1 + len(extra)),
        out_specs=vmem,
        cost_estimate=pl.CostEstimate(flops=4 * count * SEG * 16 * HD * HD, bytes_accessed=(4 + count + 2) << 20, transcendentals=0),
        compiler_params=pltpu.CompilerParams(vmem_limit_bytes=28 << 20),
        name="out",
    )(order, *flat, weight, *extra)


def per_device(tokens, norm_gain, wq, wk, wv, wo, gate_bias, mem_init, norm_init):
    seq, head = lax.axis_index("seq"), lax.axis_index("head")
    y, z = seq // NZ, seq % NZ
    x, core = head // 2, head % 2

    wq_y = jnp.stack([wq, y_move(wq, 1), y_move(wq, 2), y_move(wq, -1)])
    wkv = jnp.concatenate([wk, wv], axis=1)

    wo_gathered = lax.all_gather(spread_wo(wo), "seq", axis=0).reshape(NY, NZ, 4 * HD, HD)

    ahead, behind = [wkv], [wkv]
    ahead_q, behind_q = [wq_y], [wq_y]
    for _ in range(3):
        ahead.append(z_move(ahead[-1], 1))
        behind.append(z_move(behind[-1], -1))
        ahead_q.append(z_move(ahead_q[-1], 1))
        behind_q.append(z_move(behind_q[-1], -1))
    far = z_move(ahead[-1], 1)
    far_q = [z_move(ahead_q[-1][:2], 1), z_move(behind_q[-1][2:], -1)]
    wkv_z = jnp.stack([*ahead, far, *behind[:0:-1]])
    wkv_pieces = [wkv_z, y_move(wkv_z, 1), y_move(wkv_z, 2), y_move(wkv_z, -1)]
    wq_pieces = [*ahead_q, *far_q, *behind_q[:0:-1]]

    o_index, e_index = jnp.arange(SEQ) // NY, jnp.arange(SEQ) % NY
    order = ((y - e_index) % NY * NZ + (z - o_index) % NZ).astype(jnp.int32)
    normed = norm_call(tokens, norm_gain, order)
    queries, keys, values, delta = qkv_call(normed, wq_pieces, wkv_pieces)

    total = delta[0] + delta[1]
    before = jnp.concatenate([mem_init[0], jnp.broadcast_to(norm_init, (8, HD))], axis=0)
    for bit in (1, 2, 4):
        other = z_swap(total.astype(BF16), bit).astype(F32)
        before = before + jnp.where((z & bit) > 0, other, 0.0)
        total = total + other
    narrow = total.astype(BF16)
    for e, other in ((1, y_move(narrow, 1)), (2, y_move(narrow, 2)), (3, y_move(narrow, -1))):
        before = before + jnp.where(y >= e, other.astype(F32), 0.0)

    local = local_call(queries, keys, values)
    gate = jax.nn.sigmoid(gate_bias)
    own = [
        mix_call(gate, queries, local, before, 0),
        mix_call(gate, queries, local, before + delta[0], 1),
    ]

    left = [x_move(part, 1) for part in own]
    right = [x_move(part, -1) for part in own]
    opposite = [x_move(left[0], 1), x_move(right[1], -1)]

    def both(piece):
        return [piece, [core_swap(part) for part in piece]]

    def rows_of(distance):
        index = (x - distance) % NX * 2
        return [index + core, index + 1 - core]

    near = jnp.stack([*rows_of(0), *rows_of(1), *rows_of(-1)]).astype(jnp.int32)
    far_rows = jnp.stack(rows_of(2)).astype(jnp.int32)
    so_far = out_call(near, [*both(own), *both(left), *both(right)], wo_gathered)
    return out_call(far_rows, both(opposite), wo_gathered, so_far)


def solution(mesh):
    placed = (
        P("seq", None),
        P(),
        P("seq", "head"),
        P("seq", "head"),
        P("seq", "head"),
        P("head", "seq"),
        P("head"),
        P("head", None, None),
        P("head", None),
    )
    return jax.shard_map(
        per_device, mesh=mesh, in_specs=placed, out_specs=P("seq", "head"), check_vma=False
    )
```

```python
import functools
import math

import jax
import jax.numpy as jnp
from jax import lax
from jax.experimental import pallas as pl
from jax.experimental.pallas import tpu as pltpu
from jax.sharding import PartitionSpec as P

HD = 128
SEG = 512
NY, NZ, NX = 4, 8, 4
SEQ = NY * NZ
HEADS = 2 * NX
F32 = jnp.float32
BF16 = jnp.bfloat16
VMEM_LIMIT = 20 << 20
VMEM_MOST = 32 << 20


def z_move(block, distance):
    return lax.ppermute(
        block, "seq", [(y * NZ + z, y * NZ + (z + distance) % NZ) for y in range(NY) for z in range(NZ)]
    )


def z_swap(block, bit):
    return lax.ppermute(block, "seq", [(s, s ^ bit) for s in range(SEQ)])


def y_move(block, distance):
    return lax.ppermute(
        block, "seq", [(y * NZ + z, (y + distance) % NY * NZ + z) for y in range(NY) for z in range(NZ)]
    )


def z_gather(block):
    return lax.all_gather(block, "seq", axis=0, axis_index_groups=[[y * NZ + z for z in range(NZ)] for y in range(NY)])


def x_move(block, distance):
    return lax.ppermute(
        block, "head", [(2 * x + c, 2 * ((x + distance) % NX) + c) for x in range(NX) for c in range(2)]
    )


def core_swap(block):
    return lax.ppermute(block, "head", [(h, h ^ 1) for h in range(HEADS)])


def spread_wo(block):
    pairs = []
    for y in range(NY):
        for z in range(NZ):
            for h in range(HEADS):
                pairs.append(((4 * h + y) * HEADS + z, (y * NZ + z) * HEADS + h))
    return lax.ppermute(block, ("seq", "head"), pairs)


def feature_map(values_in):
    return jnp.where(values_in > 0, values_in + 1.0, jnp.exp(jnp.minimum(values_in, 0.0)))


def split(wide):
    high = wide.astype(BF16)
    return high, (wide - high.astype(F32)).astype(BF16)


def norm_kernel(order, x_ref, gain_ref, out_ref):
    wide = x_ref[...].astype(F32)
    scale = lax.rsqrt(jnp.mean(wide * wide, axis=-1, keepdims=True) + 1e-05)
    for block in range(SEQ):
        at = pl.ds(pl.multiple_of(order[block] * HD, HD), HD)
        part = x_ref[:, at].astype(F32) * scale * gain_ref[:, at]
        out_ref[:, block * HD : (block + 1) * HD] = part.astype(BF16)


def norm_call(tokens, gain, order):
    rows, width = tokens.shape
    tile = 128
    return pl.pallas_call(
        norm_kernel,
        out_shape=jax.ShapeDtypeStruct((rows, width), BF16),
        grid_spec=pltpu.PrefetchScalarGridSpec(
            num_scalar_prefetch=1,
            grid=(rows // tile,),
            in_specs=[
                pl.BlockSpec((tile, width), lambda i, o: (i, 0)),
                pl.BlockSpec((1, width), lambda i, o: (0, 0)),
            ],
            out_specs=pl.BlockSpec((tile, width), lambda i, o: (i, 0)),
        ),
        cost_estimate=pl.CostEstimate(flops=6 * rows * width, bytes_accessed=4 * rows * width, transcendentals=rows),
        name="norm",
    )(order, tokens, gain.reshape(1, width))


def fetch(sources, targets, sems):
    copies = [pltpu.make_async_copy(s, t, sems.at[n]) for n, (s, t) in enumerate(zip(sources, targets))]

    @pl.when(pl.program_id(0) == 0)
    def _():
        for copy in copies:
            copy.start()

    return copies


def arrived(copy):
    @pl.when(pl.program_id(0) == 0)
    def _():
        copy.wait()


COLUMNS = 4


def column_blocks(tile, width):
    return [pl.BlockSpec((tile, width // COLUMNS), lambda i, n=n: (i, n)) for n in range(COLUMNS)]


def q_kernel(*refs):
    x_refs, (w_ref, q_ref, held, sems) = refs[:COLUMNS], refs[COLUMNS:]
    size = SEQ // COLUMNS
    parts = [pl.ds(n * size, size) for n in range(COLUMNS)]
    copies = fetch([w_ref.at[part] for part in parts], [held.at[part] for part in parts], sems)
    wide = None
    for n, (copy, x_ref) in enumerate(zip(copies, x_refs)):
        arrived(copy)
        weight = held[n * size : (n + 1) * size].reshape(size * HD, 4 * HD)
        term = jnp.dot(x_ref[...], weight, preferred_element_type=F32)
        wide = term if wide is None else wide + term
    q_ref[...] = wide.astype(BF16)


def q_call(normed, weight):
    rows, width = normed.shape
    tile = 256
    return pl.pallas_call(
        q_kernel,
        grid=(rows // tile,),
        out_shape=jax.ShapeDtypeStruct((rows, 4 * HD), BF16),
        in_specs=[*column_blocks(tile, width), pl.BlockSpec(memory_space=pltpu.HBM)],
        out_specs=pl.BlockSpec((tile, 4 * HD), lambda i: (i, 0)),
        scratch_shapes=[pltpu.VMEM((SEQ, HD, 4 * HD), BF16), pltpu.SemaphoreType.DMA((COLUMNS,))],
        cost_estimate=pl.CostEstimate(flops=2 * rows * width * 4 * HD, bytes_accessed=12 << 20, transcendentals=0),
        compiler_params=pltpu.CompilerParams(vmem_limit_bytes=VMEM_MOST),
        name="q",
    )(*[normed] * COLUMNS, weight)


def kv_kernel(*refs):
    x_refs, pieces = refs[:COLUMNS], refs[COLUMNS : COLUMNS + NY]
    k_ref, v_ref, delta_ref, held, sems = refs[COLUMNS + NY :]
    each = NZ // COLUMNS
    copies = fetch(pieces, [held.at[e] for e in range(NY)], sems)
    wide = None
    for e in range(NY):
        arrived(copies[e])
        columns = jnp.concatenate(
            [x_refs[o // each][:, (o % each * NY + e) * HD : (o % each * NY + e + 1) * HD] for o in range(NZ)],
            axis=1,
        )
        term = jnp.dot(columns, held[e].reshape(NZ * HD, 2 * HD), preferred_element_type=F32)
        wide = term if wide is None else wide + term
    keys = wide[:, :HD].astype(BF16)
    values = wide[:, HD:].astype(BF16)
    k_ref[...] = keys
    v_ref[...] = values
    feats = feature_map(keys.astype(F32))
    high, low = split(feats)
    by_rows = (((0,), (0,)), ((), ()))
    memory = lax.dot_general(high, values, by_rows, preferred_element_type=F32)
    memory += lax.dot_general(low, values, by_rows, preferred_element_type=F32)
    delta_ref[0, :HD, :] = memory
    delta_ref[0, HD:, :] = jnp.broadcast_to(jnp.sum(feats, axis=0, keepdims=True), (8, HD))


def kv_call(normed, pieces):
    rows, width = normed.shape
    segments = rows // SEG
    row_block = lambda n: pl.BlockSpec((SEG, n), lambda i: (i, 0))
    return pl.pallas_call(
        kv_kernel,
        grid=(segments,),
        out_shape=[
            jax.ShapeDtypeStruct((rows, HD), BF16),
            jax.ShapeDtypeStruct((rows, HD), BF16),
            jax.ShapeDtypeStruct((segments, HD + 8, HD), F32),
        ],
        in_specs=[*column_blocks(SEG, width), *[pl.BlockSpec(memory_space=pltpu.HBM)] * len(pieces)],
        out_specs=[row_block(HD), row_block(HD), pl.BlockSpec((1, HD + 8, HD), lambda i: (i, 0, 0))],
        scratch_shapes=[pltpu.VMEM((NY, NZ, HD, 2 * HD), BF16), pltpu.SemaphoreType.DMA((NY,))],
        cost_estimate=pl.CostEstimate(flops=2 * rows * width * 2 * HD, bytes_accessed=10 << 20, transcendentals=rows * HD),
        compiler_params=pltpu.CompilerParams(vmem_limit_bytes=VMEM_MOST),
        name="kv",
    )(*[normed] * COLUMNS, *pieces)


def local_kernel(q_ref, k_ref, v_ref, out_ref):
    scale = 1.0 / math.sqrt(HD)
    half = SEG // 2
    transposed = (((1,), (1,)), ((), ()))
    for head in range(4):
        for part in range(2):
            rows = slice(part * half, (part + 1) * half)
            seen = (part + 1) * half
            query = q_ref[rows, head * HD : (head + 1) * HD]
            scores = lax.dot_general(query, k_ref[:seen, :], transposed, preferred_element_type=F32) * scale
            row = lax.broadcasted_iota(jnp.int32, (half, seen), 0) + part * half
            column = lax.broadcasted_iota(jnp.int32, (half, seen), 1)
            scores = jnp.where(row >= column, scores, -1e30)
            expd = jnp.exp(scores - jnp.max(scores, axis=-1, keepdims=True))
            probs = (expd / jnp.sum(expd, axis=-1, keepdims=True)).astype(BF16)
            out_ref[rows, head * HD : (head + 1) * HD] = jnp.dot(
                probs, v_ref[:seen, :], preferred_element_type=F32
            )


def local_call(queries, keys, values, segment):
    row_block = lambda n: pl.BlockSpec((SEG, n), lambda i: (segment, 0))
    return pl.pallas_call(
        local_kernel,
        grid=(1,),
        out_shape=jax.ShapeDtypeStruct((SEG, 4 * HD), F32),
        in_specs=[row_block(4 * HD), row_block(HD), row_block(HD)],
        out_specs=pl.BlockSpec((SEG, 4 * HD), lambda i: (0, 0)),
        cost_estimate=pl.CostEstimate(flops=16 * SEG * SEG * HD, bytes_accessed=2 << 20, transcendentals=4 * SEG * SEG),
        compiler_params=pltpu.CompilerParams(vmem_limit_bytes=VMEM_LIMIT),
        name="local",
    )(queries, keys, values)


def mix_kernel(gate_ref, q_ref, local_ref, memory_ref, out_ref):
    memory = memory_ref[:HD, :]
    normer = jnp.broadcast_to(memory_ref[HD : HD + 1, :], (HD, HD)).T
    both_high, both_low = split(jnp.concatenate([memory, normer], axis=1))
    for head in range(4):
        at = slice(head * HD, (head + 1) * HD)
        high, low = split(feature_map(q_ref[:, at].astype(F32)))
        both = jnp.dot(high, both_high, preferred_element_type=F32)
        both += jnp.dot(high, both_low, preferred_element_type=F32)
        both += jnp.dot(low, both_high, preferred_element_type=F32)
        gate = gate_ref[head]
        mixed = gate * (both[:, :HD] / both[:, HD:]) + (1.0 - gate) * local_ref[:, at]
        out_ref[:, at] = mixed.astype(BF16)


def mix_call(gate, queries, local, memory, segment):
    row_block = pl.BlockSpec((SEG, 4 * HD), lambda i: (segment, 0))
    return pl.pallas_call(
        mix_kernel,
        grid=(1,),
        out_shape=jax.ShapeDtypeStruct((SEG, 4 * HD), BF16),
        in_specs=[
            pl.BlockSpec(memory_space=pltpu.SMEM),
            row_block,
            pl.BlockSpec((SEG, 4 * HD), lambda i: (0, 0)),
            pl.BlockSpec((HD + 8, HD), lambda i: (0, 0)),
        ],
        out_specs=pl.BlockSpec((SEG, 4 * HD), lambda i: (0, 0)),
        cost_estimate=pl.CostEstimate(flops=48 * SEG * HD * HD, bytes_accessed=2 << 20, transcendentals=4 * SEG * HD),
        compiler_params=pltpu.CompilerParams(vmem_limit_bytes=16 << 20),
        name="mix",
    )(gate, queries, local, memory)


def out_kernel(count, order, *refs):
    mixed_refs, (w_hbm, out_ref, rest_ref, weights, sems) = refs[: 2 * count], refs[2 * count :]
    copies = []
    for p in range(count + 2):
        target = weights.at[p] if p < count else rest_ref.at[p - count]
        mine = [
            pltpu.make_async_copy(
                w_hbm.at[order[p], order[count + 2 + j]], target.at[:, j * HD : (j + 1) * HD], sems.at[p, j]
            )
            for j in range(NY)
        ]
        for copy in mine:
            copy.start()
        copies.append(mine)
    totals = [None, None]
    for p in range(count):
        for copy in copies[p]:
            copy.wait()
        for s in range(2):
            term = jnp.dot(mixed_refs[2 * p + s][...], weights[p], preferred_element_type=F32)
            totals[s] = term if totals[s] is None else totals[s] + term
    for s in range(2):
        out_ref[s * SEG : (s + 1) * SEG, :] = totals[s]
    for mine in copies[count:]:
        for copy in mine:
            copy.wait()


def out_call(order, pieces, weight):
    count = len(pieces)
    vmem = pl.BlockSpec(memory_space=pltpu.VMEM)
    return pl.pallas_call(
        functools.partial(out_kernel, count),
        out_shape=[
            jax.ShapeDtypeStruct((2 * SEG, 4 * HD), F32),
            jax.ShapeDtypeStruct((2, 4 * HD, 4 * HD), BF16),
        ],
        in_specs=[
            pl.BlockSpec(memory_space=pltpu.SMEM),
            *[vmem] * (2 * count),
            pl.BlockSpec(memory_space=pltpu.HBM),
        ],
        out_specs=[vmem, vmem],
        scratch_shapes=[
            pltpu.VMEM((count, 4 * HD, 4 * HD), BF16),
            pltpu.SemaphoreType.DMA((count + 2, NY)),
        ],
        cost_estimate=pl.CostEstimate(flops=4 * count * SEG * 16 * HD * HD, bytes_accessed=(2 * count + 4) << 20, transcendentals=0),
        compiler_params=pltpu.CompilerParams(vmem_limit_bytes=VMEM_LIMIT),
        name="out",
    )(order, *[part for piece in pieces for part in piece], weight)


def add_kernel(which, mixed_0, mixed_1, w_ref, so_far, out_ref):
    for s, mixed_ref in enumerate((mixed_0, mixed_1)):
        at = slice(s * SEG, (s + 1) * SEG)
        term = jnp.dot(mixed_ref[...], w_ref[which], preferred_element_type=F32)
        out_ref[at, :] = (so_far[at, :] + term).astype(out_ref.dtype)


def add_call(which, piece, weights, so_far, dtype):
    vmem = pl.BlockSpec(memory_space=pltpu.VMEM)
    return pl.pallas_call(
        functools.partial(add_kernel, which),
        out_shape=jax.ShapeDtypeStruct(so_far.shape, dtype),
        in_specs=[vmem] * 4,
        out_specs=vmem,
        cost_estimate=pl.CostEstimate(flops=4 * SEG * 16 * HD * HD, bytes_accessed=4 << 20, transcendentals=0),
        compiler_params=pltpu.CompilerParams(vmem_limit_bytes=VMEM_LIMIT),
        name="add",
    )(*piece, weights, so_far)


def per_device(tokens, norm_gain, wq, wk, wv, wo, gate_bias, mem_init, norm_init):
    seq, head = lax.axis_index("seq"), lax.axis_index("head")
    y, z = seq // NZ, seq % NZ
    x, core = head // 2, head % 2

    together = lax.optimization_barrier
    z_index, e_index = jnp.arange(SEQ) // NY, jnp.arange(SEQ) % NY
    order = ((y - e_index) % NY * NZ + z_index).astype(jnp.int32)

    wkv = jnp.concatenate([wk, wv], axis=1)
    wq_1, wq_2, wq_3 = y_move(wq, 1), y_move(wq, 2), y_move(wq, -1)
    one, back = z_move(wkv, 1), z_move(wkv, -1)
    wo_own = spread_wo(wo)
    wq_1, wq_2, wq_3, one, back, wo_own = together((wq_1, wq_2, wq_3, one, back, wo_own))
    wq_y = jnp.stack([wq, wq_1, wq_2, wq_3])
    wq_gathered = z_gather(wq_y)
    trio = jnp.stack([back, wkv, one])
    wkv_p, wkv_m = z_move(trio, 3), z_move(trio[1:], -3)
    wkv_z = jnp.concatenate(
        [wkv[None], back[None], wkv_m[1:], wkv_m[:1], wkv_p[2:], wkv_p[1:2], wkv_p[:1], one[None]]
    )
    wkv_z = lax.dynamic_slice_in_dim(jnp.concatenate([wkv_z, wkv_z[:-1]]), (NZ - z) % NZ, NZ)
    wo_y = jnp.stack([wo_own, y_move(wo_own, 1), y_move(wo_own, 2), y_move(wo_own, -1)])
    wkv_z, wo_y = together((wkv_z, wo_y))
    wkv_pieces = [wkv_z, y_move(wkv_z, 1), y_move(wkv_z, 2), y_move(wkv_z, -1)]
    normed = norm_call(tokens, norm_gain, order)
    keys, values, delta = kv_call(normed, wkv_pieces)
    wo_gathered = z_gather(wo_y)
    total = delta[0] + delta[1]
    before = jnp.concatenate([mem_init[0], jnp.broadcast_to(norm_init, (8, HD))], axis=0)
    for bit in (1, 2, 4):
        other = z_swap(total.astype(BF16), bit).astype(F32)
        before = before + jnp.where((z & bit) > 0, other, 0.0)
        total = total + other
    total, wq_gathered = together((total, wq_gathered))
    queries = q_call(normed, wq_gathered.reshape(SEQ, HD, 4 * HD))
    narrow = total.astype(BF16)
    for e, other in ((1, y_move(narrow, 1)), (2, y_move(narrow, 2)), (3, y_move(narrow, -1))):
        before = before + jnp.where(y >= e, other.astype(F32), 0.0)

    gate = jax.nn.sigmoid(gate_bias)
    local = [local_call(queries, keys, values, segment) for segment in range(2)]
    own = [
        mix_call(gate, queries, local[0], before, 0),
        mix_call(gate, queries, local[1], before + delta[0], 1),
    ]

    left = [x_move(own[0], 1)]
    right = [x_move(own[0], -1)]
    left.append(x_move(own[1], 1))
    right.append(x_move(own[1], -1))
    opposite = [x_move(left[0], 1), x_move(right[1], -1)]
    own_swapped = [core_swap(part) for part in own]

    def both(piece):
        return [piece, [core_swap(part) for part in piece]]

    def rows_of(distance):
        index = (x - distance) % NX * 2
        return [index + core, index + 1 - core]

    blocks = [(y - j) % NY for j in range(NY)]
    at = jnp.stack([row for d in (0, 1, -1, 2) for row in rows_of(d)] + blocks).astype(jnp.int32)
    near = [own, own_swapped, *both(left), *both(right)]
    so_far, rest = out_call(at, near, wo_gathered)
    opposite[0], opposite[1], so_far = together((opposite[0], opposite[1], so_far))
    swapped = [core_swap(part) for part in opposite]
    so_far = add_call(0, opposite, rest, so_far, F32)
    swapped[0], swapped[1], so_far = together((swapped[0], swapped[1], so_far))
    return add_call(1, swapped, rest, so_far, BF16)


def solution(mesh):
    placed = (
        P("seq", None),
        P(),
        P("seq", "head"),
        P("seq", "head"),
        P("seq", "head"),
        P("head", "seq"),
        P("head"),
        P("head", None, None),
        P("head", None),
    )
    return jax.shard_map(
        per_device, mesh=mesh, in_specs=placed, out_specs=P("seq", "head"), check_vma=False
    )
```

```python
import functools
import math

import jax
import jax.numpy as jnp
from jax import lax
from jax.experimental import pallas as pl
from jax.experimental.pallas import tpu as pltpu
from jax.sharding import PartitionSpec as P

HD = 128
SEG = 512
NY, NZ, NX = 4, 8, 4
SEQ = NY * NZ
HEADS = 2 * NX
F32 = jnp.float32
BF16 = jnp.bfloat16
VMEM_LIMIT = 20 << 20
VMEM_MOST = 32 << 20


def z_move(block, distance):
    return lax.ppermute(
        block, "seq", [(y * NZ + z, y * NZ + (z + distance) % NZ) for y in range(NY) for z in range(NZ)]
    )


def z_swap(block, bit):
    return lax.ppermute(block, "seq", [(s, s ^ bit) for s in range(SEQ)])


def y_move(block, distance):
    return lax.ppermute(
        block, "seq", [(y * NZ + z, (y + distance) % NY * NZ + z) for y in range(NY) for z in range(NZ)]
    )


def z_gather(block):
    return lax.all_gather(block, "seq", axis=0, axis_index_groups=[[y * NZ + z for z in range(NZ)] for y in range(NY)])


def x_move(block, distance):
    return lax.ppermute(
        block, "head", [(2 * x + c, 2 * ((x + distance) % NX) + c) for x in range(NX) for c in range(2)]
    )


def core_swap(block):
    return lax.ppermute(block, "head", [(h, h ^ 1) for h in range(HEADS)])


def spread_wo(block):
    pairs = []
    for y in range(NY):
        for z in range(NZ):
            for h in range(HEADS):
                pairs.append(((4 * h + y) * HEADS + z, (y * NZ + z) * HEADS + h))
    return lax.ppermute(block, ("seq", "head"), pairs)


def feature_map(values_in):
    return jnp.where(values_in > 0, values_in + 1.0, jnp.exp(jnp.minimum(values_in, 0.0)))


def split(wide):
    high = wide.astype(BF16)
    return high, (wide - high.astype(F32)).astype(BF16)


def norm_kernel(order, x_ref, gain_ref, out_ref):
    wide = x_ref[...].astype(F32)
    scale = lax.rsqrt(jnp.mean(wide * wide, axis=-1, keepdims=True) + 1e-05)
    for block in range(SEQ):
        at = pl.ds(pl.multiple_of(order[block] * HD, HD), HD)
        part = x_ref[:, at].astype(F32) * scale * gain_ref[:, at]
        out_ref[:, block * HD : (block + 1) * HD] = part.astype(BF16)


def norm_call(tokens, gain, order):
    rows, width = tokens.shape
    tile = 128
    return pl.pallas_call(
        norm_kernel,
        out_shape=jax.ShapeDtypeStruct((rows, width), BF16),
        grid_spec=pltpu.PrefetchScalarGridSpec(
            num_scalar_prefetch=1,
            grid=(rows // tile,),
            in_specs=[
                pl.BlockSpec((tile, width), lambda i, o: (i, 0)),
                pl.BlockSpec((1, width), lambda i, o: (0, 0)),
            ],
            out_specs=pl.BlockSpec((tile, width), lambda i, o: (i, 0)),
        ),
        cost_estimate=pl.CostEstimate(flops=6 * rows * width, bytes_accessed=4 * rows * width, transcendentals=rows),
        name="norm",
    )(order, tokens, gain.reshape(1, width))


def fetch(sources, targets, sems):
    copies = [pltpu.make_async_copy(s, t, sems.at[n]) for n, (s, t) in enumerate(zip(sources, targets))]

    @pl.when(pl.program_id(0) == 0)
    def _():
        for copy in copies:
            copy.start()

    return copies


def arrived(copy):
    @pl.when(pl.program_id(0) == 0)
    def _():
        copy.wait()


COLUMNS = 4


def column_blocks(tile, width):
    return [pl.BlockSpec((tile, width // COLUMNS), lambda i, n=n: (i, n)) for n in range(COLUMNS)]


def q_kernel(*refs):
    x_refs, (w_ref, q_ref, held, sems) = refs[:COLUMNS], refs[COLUMNS:]
    size = SEQ // COLUMNS
    parts = [pl.ds(n * size, size) for n in range(COLUMNS)]
    copies = fetch([w_ref.at[part] for part in parts], [held.at[part] for part in parts], sems)
    wide = None
    for n, (copy, x_ref) in enumerate(zip(copies, x_refs)):
        arrived(copy)
        weight = held[n * size : (n + 1) * size].reshape(size * HD, 4 * HD)
        term = jnp.dot(x_ref[...], weight, preferred_element_type=F32)
        wide = term if wide is None else wide + term
    q_ref[...] = wide.astype(BF16)


def q_call(normed, weight):
    rows, width = normed.shape
    tile = 256
    return pl.pallas_call(
        q_kernel,
        grid=(rows // tile,),
        out_shape=jax.ShapeDtypeStruct((rows, 4 * HD), BF16),
        in_specs=[*column_blocks(tile, width), pl.BlockSpec(memory_space=pltpu.HBM)],
        out_specs=pl.BlockSpec((tile, 4 * HD), lambda i: (i, 0)),
        scratch_shapes=[pltpu.VMEM((SEQ, HD, 4 * HD), BF16), pltpu.SemaphoreType.DMA((COLUMNS,))],
        cost_estimate=pl.CostEstimate(flops=2 * rows * width * 4 * HD, bytes_accessed=12 << 20, transcendentals=0),
        compiler_params=pltpu.CompilerParams(vmem_limit_bytes=56 << 20),
        name="q",
    )(*[normed] * COLUMNS, weight)


def kv_kernel(*refs):
    x_refs, pieces = refs[:COLUMNS], refs[COLUMNS : COLUMNS + NY]
    k_ref, v_ref, delta_ref, held, sems = refs[COLUMNS + NY :]
    copies = fetch([piece.at[pl.ds(0, NZ)] for piece in pieces], [held.at[:, e] for e in range(NY)], sems)
    for copy in copies:
        arrived(copy)
    each = NZ // COLUMNS
    wide = None
    for n, x_ref in enumerate(x_refs):
        weight = held[n * each : (n + 1) * each].reshape(each * NY * HD, 2 * HD)
        term = jnp.dot(x_ref[...], weight, preferred_element_type=F32)
        wide = term if wide is None else wide + term
    keys = wide[:, :HD].astype(BF16)
    values = wide[:, HD:].astype(BF16)
    k_ref[...] = keys
    v_ref[...] = values
    feats = feature_map(keys.astype(F32))
    high, low = split(feats)
    by_rows = (((0,), (0,)), ((), ()))
    memory = lax.dot_general(high, values, by_rows, preferred_element_type=F32)
    memory += lax.dot_general(low, values, by_rows, preferred_element_type=F32)
    norm = jnp.broadcast_to(jnp.sum(feats, axis=0, keepdims=True), (8, HD))

    @pl.when(pl.program_id(0) % 2 == 0)
    def _():
        delta_ref[0, :HD, :] = memory
        delta_ref[0, HD:, :] = norm

    @pl.when(pl.program_id(0) % 2 == 1)
    def _():
        delta_ref[0, :HD, :] += memory
        delta_ref[0, HD:, :] += norm


def kv_call(normed, pieces):
    rows, width = normed.shape
    tile = SEG // 2
    row_block = pl.BlockSpec((tile, HD), lambda i: (i, 0))
    return pl.pallas_call(
        kv_kernel,
        grid=(rows // tile,),
        out_shape=[
            jax.ShapeDtypeStruct((rows, HD), BF16),
            jax.ShapeDtypeStruct((rows, HD), BF16),
            jax.ShapeDtypeStruct((rows // SEG, HD + 8, HD), F32),
        ],
        in_specs=[*column_blocks(tile, width), *[pl.BlockSpec(memory_space=pltpu.HBM)] * len(pieces)],
        out_specs=[row_block, row_block, pl.BlockSpec((1, HD + 8, HD), lambda i: (i // 2, 0, 0))],
        scratch_shapes=[pltpu.VMEM((NZ, NY, HD, 2 * HD), BF16), pltpu.SemaphoreType.DMA((NY,))],
        cost_estimate=pl.CostEstimate(flops=2 * rows * width * 2 * HD, bytes_accessed=10 << 20, transcendentals=rows * HD),
        compiler_params=pltpu.CompilerParams(vmem_limit_bytes=VMEM_MOST),
        name="kv",
    )(*[normed] * COLUMNS, *pieces)


def local_kernel(q_ref, k_ref, v_ref, out_ref):
    scale = 1.0 / math.sqrt(HD)
    half = SEG // 2
    transposed = (((1,), (1,)), ((), ()))
    for head in range(4):
        for part in range(2):
            rows = slice(part * half, (part + 1) * half)
            seen = (part + 1) * half
            query = q_ref[rows, head * HD : (head + 1) * HD]
            scores = lax.dot_general(query, k_ref[:seen, :], transposed, preferred_element_type=F32) * scale
            row = lax.broadcasted_iota(jnp.int32, (half, seen), 0) + part * half
            column = lax.broadcasted_iota(jnp.int32, (half, seen), 1)
            scores = jnp.where(row >= column, scores, -1e30)
            expd = jnp.exp(scores - jnp.max(scores, axis=-1, keepdims=True))
            probs = (expd / jnp.sum(expd, axis=-1, keepdims=True)).astype(BF16)
            out_ref[rows, head * HD : (head + 1) * HD] = jnp.dot(
                probs, v_ref[:seen, :], preferred_element_type=F32
            )


def local_call(queries, keys, values, segment):
    row_block = lambda n: pl.BlockSpec((SEG, n), lambda i: (segment, 0))
    return pl.pallas_call(
        local_kernel,
        grid=(1,),
        out_shape=jax.ShapeDtypeStruct((SEG, 4 * HD), F32),
        in_specs=[row_block(4 * HD), row_block(HD), row_block(HD)],
        out_specs=pl.BlockSpec((SEG, 4 * HD), lambda i: (0, 0)),
        cost_estimate=pl.CostEstimate(flops=16 * SEG * SEG * HD, bytes_accessed=2 << 20, transcendentals=4 * SEG * SEG),
        compiler_params=pltpu.CompilerParams(vmem_limit_bytes=VMEM_LIMIT),
        name="local",
    )(queries, keys, values)


def mix_kernel(gate_ref, q_ref, local_ref, memory_ref, out_ref):
    memory = memory_ref[:HD, :]
    normer = jnp.broadcast_to(memory_ref[HD : HD + 1, :], (HD, HD)).T
    both_high, both_low = split(jnp.concatenate([memory, normer], axis=1))
    for head in range(4):
        at = slice(head * HD, (head + 1) * HD)
        high, low = split(feature_map(q_ref[:, at].astype(F32)))
        both = jnp.dot(high, both_high, preferred_element_type=F32)
        both += jnp.dot(high, both_low, preferred_element_type=F32)
        both += jnp.dot(low, both_high, preferred_element_type=F32)
        gate = gate_ref[head]
        mixed = gate * (both[:, :HD] / both[:, HD:]) + (1.0 - gate) * local_ref[:, at]
        out_ref[:, at] = mixed.astype(BF16)


def mix_call(gate, queries, local, memory, segment):
    row_block = pl.BlockSpec((SEG, 4 * HD), lambda i: (segment, 0))
    return pl.pallas_call(
        mix_kernel,
        grid=(1,),
        out_shape=jax.ShapeDtypeStruct((SEG, 4 * HD), BF16),
        in_specs=[
            pl.BlockSpec(memory_space=pltpu.SMEM),
            row_block,
            pl.BlockSpec((SEG, 4 * HD), lambda i: (0, 0)),
            pl.BlockSpec((HD + 8, HD), lambda i: (0, 0)),
        ],
        out_specs=pl.BlockSpec((SEG, 4 * HD), lambda i: (0, 0)),
        cost_estimate=pl.CostEstimate(flops=48 * SEG * HD * HD, bytes_accessed=2 << 20, transcendentals=4 * SEG * HD),
        compiler_params=pltpu.CompilerParams(vmem_limit_bytes=16 << 20),
        name="mix",
    )(gate, queries, local, memory)


def out_kernel(count, order, *refs):
    mixed_refs, (w_hbm, out_ref, rest_ref, weights, sems) = refs[: 2 * count], refs[2 * count :]
    copies = []
    for p in range(count + 2):
        target = weights.at[p] if p < count else rest_ref.at[p - count]
        mine = [
            pltpu.make_async_copy(
                w_hbm.at[order[p], order[count + 2 + j], :, n * HD : (n + 1) * HD],
                target.at[n * 2 * HD : (n + 1) * 2 * HD, j * HD : (j + 1) * HD],
                sems.at[p, 2 * j + n],
            )
            for j in range(NY)
            for n in range(2)
        ]
        for copy in mine:
            copy.start()
        copies.append(mine)
    totals = [None, None]
    for p in range(count):
        for copy in copies[p]:
            copy.wait()
        for s in range(2):
            term = jnp.dot(mixed_refs[2 * p + s][...], weights[p], preferred_element_type=F32)
            totals[s] = term if totals[s] is None else totals[s] + term
    for s in range(2):
        out_ref[s * SEG : (s + 1) * SEG, :] = totals[s]
    for mine in copies[count:]:
        for copy in mine:
            copy.wait()


def out_call(order, pieces, weight):
    count = len(pieces)
    vmem = pl.BlockSpec(memory_space=pltpu.VMEM)
    return pl.pallas_call(
        functools.partial(out_kernel, count),
        out_shape=[
            jax.ShapeDtypeStruct((2 * SEG, 4 * HD), F32),
            jax.ShapeDtypeStruct((2, 4 * HD, 4 * HD), BF16),
        ],
        in_specs=[
            pl.BlockSpec(memory_space=pltpu.SMEM),
            *[vmem] * (2 * count),
            pl.BlockSpec(memory_space=pltpu.HBM),
        ],
        out_specs=[vmem, vmem],
        scratch_shapes=[
            pltpu.VMEM((count, 4 * HD, 4 * HD), BF16),
            pltpu.SemaphoreType.DMA((count + 2, 2 * NY)),
        ],
        cost_estimate=pl.CostEstimate(flops=4 * count * SEG * 16 * HD * HD, bytes_accessed=(2 * count + 4) << 20, transcendentals=0),
        compiler_params=pltpu.CompilerParams(vmem_limit_bytes=VMEM_LIMIT),
        name="out",
    )(order, *[part for piece in pieces for part in piece], weight)


def add_kernel(which, mixed_0, mixed_1, w_ref, so_far, out_ref):
    for s, mixed_ref in enumerate((mixed_0, mixed_1)):
        at = slice(s * SEG, (s + 1) * SEG)
        term = jnp.dot(mixed_ref[...], w_ref[which], preferred_element_type=F32)
        out_ref[at, :] = (so_far[at, :] + term).astype(out_ref.dtype)


def add_call(which, piece, weights, so_far, dtype):
    vmem = pl.BlockSpec(memory_space=pltpu.VMEM)
    return pl.pallas_call(
        functools.partial(add_kernel, which),
        out_shape=jax.ShapeDtypeStruct(so_far.shape, dtype),
        in_specs=[vmem] * 4,
        out_specs=vmem,
        cost_estimate=pl.CostEstimate(flops=4 * SEG * 16 * HD * HD, bytes_accessed=4 << 20, transcendentals=0),
        compiler_params=pltpu.CompilerParams(vmem_limit_bytes=VMEM_LIMIT),
        name="add",
    )(*piece, weights, so_far)


def per_device(tokens, norm_gain, wq, wk, wv, wo, gate_bias, mem_init, norm_init):
    seq, head = lax.axis_index("seq"), lax.axis_index("head")
    y, z = seq // NZ, seq % NZ
    x, core = head // 2, head % 2

    together = lax.optimization_barrier
    z_index, e_index = jnp.arange(SEQ) // NY, jnp.arange(SEQ) % NY
    order = ((y - e_index) % NY * NZ + z_index).astype(jnp.int32)

    wkv = jnp.concatenate([wk, wv], axis=1)
    wq_1, wq_2, wq_3 = y_move(wq, 1), y_move(wq, 2), y_move(wq, -1)
    one, back = z_move(wkv, 1), z_move(wkv, -1)
    wo_own = spread_wo(wo)
    wq_1, wq_2, wq_3, one, back, wo_own = together((wq_1, wq_2, wq_3, one, back, wo_own))
    wq_y = jnp.stack([wq, wq_1, wq_2, wq_3])
    trio = jnp.stack([back, wkv, one])
    wkv_p, wkv_m = z_move(trio, 3), z_move(trio[1:], -3)
    wq_y, wkv_p, wkv_m = together((wq_y, wkv_p, wkv_m))
    wq_gathered = z_gather(wq_y)
    wkv_z = jnp.concatenate(
        [wkv[None], back[None], wkv_m[1:], wkv_m[:1], wkv_p[2:], wkv_p[1:2], wkv_p[:1], one[None]]
    )
    wkv_z = lax.dynamic_slice_in_dim(jnp.concatenate([wkv_z, wkv_z[:-1]]), (NZ - z) % NZ, NZ)
    half = wo_own.shape[0] // 2
    wo_own = jnp.concatenate([wo_own[:half], wo_own[half:]], axis=1).reshape(2, HD, 2 * HD)
    packed = jnp.concatenate([wkv_z, wo_own])
    packs = [packed, y_move(packed, 1), y_move(packed, 2), y_move(packed, -1)]
    normed = norm_call(tokens, norm_gain, order)
    *packs, normed = together((*packs, normed))
    keys, values, delta = kv_call(normed, packs)
    wo_y = jnp.stack([pack[NZ:].reshape(half, 2 * HD) for pack in packs])
    wo_gathered = z_gather(wo_y)

    total = delta[0] + delta[1]
    before = jnp.concatenate([mem_init[0], jnp.broadcast_to(norm_init, (8, HD))], axis=0)
    for bit in (1, 2, 4):
        other = z_swap(total.astype(BF16), bit).astype(F32)
        before = before + jnp.where((z & bit) > 0, other, 0.0)
        total = total + other
    total, wq_gathered = together((total, wq_gathered))
    queries = q_call(normed, wq_gathered.reshape(SEQ, HD, 4 * HD))
    narrow = total.astype(BF16)
    for e, other in ((1, y_move(narrow, 1)), (2, y_move(narrow, 2)), (3, y_move(narrow, -1))):
        before = before + jnp.where(y >= e, other.astype(F32), 0.0)

    gate = jax.nn.sigmoid(gate_bias)
    local = [local_call(queries, keys, values, segment) for segment in range(2)]
    own = [
        mix_call(gate, queries, local[0], before, 0),
        mix_call(gate, queries, local[1], before + delta[0], 1),
    ]

    left = [x_move(own[0], 1)]
    right = [x_move(own[0], -1)]
    left.append(x_move(own[1], 1))
    right.append(x_move(own[1], -1))
    opposite = [x_move(left[0], 1), x_move(right[1], -1)]
    own_swapped = [core_swap(part) for part in own]

    def both(piece):
        return [piece, [core_swap(part) for part in piece]]

    def rows_of(distance):
        index = (x - distance) % NX * 2
        return [index + core, index + 1 - core]

    blocks = [(y - j) % NY for j in range(NY)]
    at = jnp.stack([row for d in (0, 1, -1, 2) for row in rows_of(d)] + blocks).astype(jnp.int32)
    near = [own, own_swapped, *both(left), *both(right)]
    so_far, rest = out_call(at, near, wo_gathered)
    opposite[0], opposite[1], so_far = together((opposite[0], opposite[1], so_far))
    swapped = [core_swap(part) for part in opposite]
    so_far = add_call(0, opposite, rest, so_far, F32)
    swapped[0], swapped[1], so_far = together((swapped[0], swapped[1], so_far))
    return add_call(1, swapped, rest, so_far, BF16)


def solution(mesh):
    placed = (
        P("seq", None),
        P(),
        P("seq", "head"),
        P("seq", "head"),
        P("seq", "head"),
        P("head", "seq"),
        P("head"),
        P("head", None, None),
        P("head", None),
    )
    return jax.shard_map(
        per_device, mesh=mesh, in_specs=placed, out_specs=P("seq", "head"), check_vma=False
    )
```

```python
import functools
import math

import jax
import jax.numpy as jnp
from jax import lax
from jax.experimental import pallas as pl
from jax.experimental.pallas import tpu as pltpu
from jax.sharding import PartitionSpec as P

HD = 128
SEG = 512
NY, NZ, NX = 4, 8, 4
SEQ = NY * NZ
HEADS = 2 * NX
F32 = jnp.float32
BF16 = jnp.bfloat16
VMEM_LIMIT = 20 << 20
VMEM_MOST = 32 << 20


def z_move(block, distance):
    return lax.ppermute(
        block, "seq", [(y * NZ + z, y * NZ + (z + distance) % NZ) for y in range(NY) for z in range(NZ)]
    )


def z_swap(block, bit):
    return lax.ppermute(block, "seq", [(s, s ^ bit) for s in range(SEQ)])


def y_move(block, distance):
    return lax.ppermute(
        block, "seq", [(y * NZ + z, (y + distance) % NY * NZ + z) for y in range(NY) for z in range(NZ)]
    )


def z_gather(block):
    return lax.all_gather(block, "seq", axis=0, axis_index_groups=[[y * NZ + z for z in range(NZ)] for y in range(NY)])


def x_move(block, distance):
    return lax.ppermute(
        block, "head", [(2 * x + c, 2 * ((x + distance) % NX) + c) for x in range(NX) for c in range(2)]
    )


def core_swap(block):
    return lax.ppermute(block, "head", [(h, h ^ 1) for h in range(HEADS)])


def spread_wo(block):
    pairs = []
    for y in range(NY):
        for z in range(NZ):
            for h in range(HEADS):
                pairs.append(((4 * h + y) * HEADS + z, (y * NZ + z) * HEADS + h))
    return lax.ppermute(block, ("seq", "head"), pairs)


def feature_map(values_in):
    return jnp.where(values_in > 0, values_in + 1.0, jnp.exp(jnp.minimum(values_in, 0.0)))


def split(wide):
    high = wide.astype(BF16)
    return high, (wide - high.astype(F32)).astype(BF16)


def norm_kernel(order, x_ref, gain_ref, out_ref):
    wide = x_ref[...].astype(F32)
    scale = lax.rsqrt(jnp.mean(wide * wide, axis=-1, keepdims=True) + 1e-05)
    for block in range(SEQ):
        at = pl.ds(pl.multiple_of(order[block] * HD, HD), HD)
        part = x_ref[:, at].astype(F32) * scale * gain_ref[:, at]
        out_ref[:, block * HD : (block + 1) * HD] = part.astype(BF16)


def norm_call(tokens, gain, order):
    rows, width = tokens.shape
    tile = 128
    return pl.pallas_call(
        norm_kernel,
        out_shape=jax.ShapeDtypeStruct((rows, width), BF16),
        grid_spec=pltpu.PrefetchScalarGridSpec(
            num_scalar_prefetch=1,
            grid=(rows // tile,),
            in_specs=[
                pl.BlockSpec((tile, width), lambda i, o: (i, 0)),
                pl.BlockSpec((1, width), lambda i, o: (0, 0)),
            ],
            out_specs=pl.BlockSpec((tile, width), lambda i, o: (i, 0)),
        ),
        cost_estimate=pl.CostEstimate(flops=6 * rows * width, bytes_accessed=4 * rows * width, transcendentals=rows),
        name="norm",
    )(order, tokens, gain.reshape(1, width))


def fetch(sources, targets, sems):
    copies = [pltpu.make_async_copy(s, t, sems.at[n]) for n, (s, t) in enumerate(zip(sources, targets))]

    @pl.when(pl.program_id(0) == 0)
    def _():
        for copy in copies:
            copy.start()

    return copies


def arrived(copy):
    @pl.when(pl.program_id(0) == 0)
    def _():
        copy.wait()


COLUMNS = 4


def column_blocks(tile, width):
    return [pl.BlockSpec((tile, width // COLUMNS), lambda i, n=n: (i, n)) for n in range(COLUMNS)]


def q_kernel(*refs):
    x_refs, (w_ref, q_ref, held, sems) = refs[:COLUMNS], refs[COLUMNS:]
    size = SEQ // COLUMNS
    parts = [pl.ds(n * size, size) for n in range(COLUMNS)]
    copies = fetch([w_ref.at[part] for part in parts], [held.at[part] for part in parts], sems)
    wide = None
    for n, (copy, x_ref) in enumerate(zip(copies, x_refs)):
        arrived(copy)
        weight = held[n * size : (n + 1) * size].reshape(size * HD, 4 * HD)
        term = jnp.dot(x_ref[...], weight, preferred_element_type=F32)
        wide = term if wide is None else wide + term
    q_ref[...] = wide.astype(BF16)


def q_call(normed, weight):
    rows, width = normed.shape
    tile = 256
    return pl.pallas_call(
        q_kernel,
        grid=(rows // tile,),
        out_shape=jax.ShapeDtypeStruct((rows, 4 * HD), BF16),
        in_specs=[*column_blocks(tile, width), pl.BlockSpec(memory_space=pltpu.HBM)],
        out_specs=pl.BlockSpec((tile, 4 * HD), lambda i: (i, 0)),
        scratch_shapes=[pltpu.VMEM((SEQ, HD, 4 * HD), BF16), pltpu.SemaphoreType.DMA((COLUMNS,))],
        cost_estimate=pl.CostEstimate(flops=2 * rows * width * 4 * HD, bytes_accessed=12 << 20, transcendentals=0),
        compiler_params=pltpu.CompilerParams(vmem_limit_bytes=56 << 20),
        name="q",
    )(*[normed] * COLUMNS, weight)


def kv_kernel(*refs):
    x_refs, pieces = refs[:COLUMNS], refs[COLUMNS : COLUMNS + NY]
    k_ref, v_ref, delta_ref, held, sems = refs[COLUMNS + NY :]
    copies = fetch(pieces, [held.at[:, e] for e in range(NY)], sems)
    for copy in copies:
        arrived(copy)
    each = NZ // COLUMNS
    wide = None
    for n, x_ref in enumerate(x_refs):
        weight = held[n * each : (n + 1) * each].reshape(each * NY * HD, 2 * HD)
        term = jnp.dot(x_ref[...], weight, preferred_element_type=F32)
        wide = term if wide is None else wide + term
    keys = wide[:, :HD].astype(BF16)
    values = wide[:, HD:].astype(BF16)
    k_ref[...] = keys
    v_ref[...] = values
    feats = feature_map(keys.astype(F32))
    high, low = split(feats)
    by_rows = (((0,), (0,)), ((), ()))
    memory = lax.dot_general(high, values, by_rows, preferred_element_type=F32)
    memory += lax.dot_general(low, values, by_rows, preferred_element_type=F32)
    norm = jnp.broadcast_to(jnp.sum(feats, axis=0, keepdims=True), (8, HD))

    @pl.when(pl.program_id(0) % 2 == 0)
    def _():
        delta_ref[0, :HD, :] = memory
        delta_ref[0, HD:, :] = norm

    @pl.when(pl.program_id(0) % 2 == 1)
    def _():
        delta_ref[0, :HD, :] += memory
        delta_ref[0, HD:, :] += norm


def kv_call(normed, pieces):
    rows, width = normed.shape
    tile = SEG // 2
    row_block = pl.BlockSpec((tile, HD), lambda i: (i, 0))
    return pl.pallas_call(
        kv_kernel,
        grid=(rows // tile,),
        out_shape=[
            jax.ShapeDtypeStruct((rows, HD), BF16),
            jax.ShapeDtypeStruct((rows, HD), BF16),
            jax.ShapeDtypeStruct((rows // SEG, HD + 8, HD), F32),
        ],
        in_specs=[*column_blocks(tile, width), *[pl.BlockSpec(memory_space=pltpu.HBM)] * len(pieces)],
        out_specs=[row_block, row_block, pl.BlockSpec((1, HD + 8, HD), lambda i: (i // 2, 0, 0))],
        scratch_shapes=[pltpu.VMEM((NZ, NY, HD, 2 * HD), BF16), pltpu.SemaphoreType.DMA((NY,))],
        cost_estimate=pl.CostEstimate(flops=2 * rows * width * 2 * HD, bytes_accessed=10 << 20, transcendentals=rows * HD),
        compiler_params=pltpu.CompilerParams(vmem_limit_bytes=VMEM_MOST),
        name="kv",
    )(*[normed] * COLUMNS, *pieces)


def local_kernel(q_ref, k_ref, v_ref, out_ref):
    scale = 1.0 / math.sqrt(HD)
    half = SEG // 2
    transposed = (((1,), (1,)), ((), ()))
    for head in range(4):
        for part in range(2):
            rows = slice(part * half, (part + 1) * half)
            seen = (part + 1) * half
            query = q_ref[rows, head * HD : (head + 1) * HD]
            scores = lax.dot_general(query, k_ref[:seen, :], transposed, preferred_element_type=F32) * scale
            row = lax.broadcasted_iota(jnp.int32, (half, seen), 0) + part * half
            column = lax.broadcasted_iota(jnp.int32, (half, seen), 1)
            scores = jnp.where(row >= column, scores, -1e30)
            expd = jnp.exp(scores - jnp.max(scores, axis=-1, keepdims=True))
            probs = (expd / jnp.sum(expd, axis=-1, keepdims=True)).astype(BF16)
            out_ref[rows, head * HD : (head + 1) * HD] = jnp.dot(
                probs, v_ref[:seen, :], preferred_element_type=F32
            )


def local_call(queries, keys, values, segment):
    row_block = lambda n: pl.BlockSpec((SEG, n), lambda i: (segment, 0))
    return pl.pallas_call(
        local_kernel,
        grid=(1,),
        out_shape=jax.ShapeDtypeStruct((SEG, 4 * HD), F32),
        in_specs=[row_block(4 * HD), row_block(HD), row_block(HD)],
        out_specs=pl.BlockSpec((SEG, 4 * HD), lambda i: (0, 0)),
        cost_estimate=pl.CostEstimate(flops=16 * SEG * SEG * HD, bytes_accessed=2 << 20, transcendentals=4 * SEG * SEG),
        compiler_params=pltpu.CompilerParams(vmem_limit_bytes=VMEM_LIMIT),
        name="local",
    )(queries, keys, values)


def mix_kernel(gate_ref, q_ref, local_ref, memory_ref, out_ref):
    memory = memory_ref[:HD, :]
    normer = jnp.broadcast_to(memory_ref[HD : HD + 1, :], (HD, HD)).T
    both_high, both_low = split(jnp.concatenate([memory, normer], axis=1))
    for head in range(4):
        at = slice(head * HD, (head + 1) * HD)
        high, low = split(feature_map(q_ref[:, at].astype(F32)))
        both = jnp.dot(high, both_high, preferred_element_type=F32)
        both += jnp.dot(high, both_low, preferred_element_type=F32)
        both += jnp.dot(low, both_high, preferred_element_type=F32)
        gate = gate_ref[head]
        mixed = gate * (both[:, :HD] / both[:, HD:]) + (1.0 - gate) * local_ref[:, at]
        out_ref[:, at] = mixed.astype(BF16)


def mix_call(gate, queries, local, memory, segment):
    row_block = pl.BlockSpec((SEG, 4 * HD), lambda i: (segment, 0))
    return pl.pallas_call(
        mix_kernel,
        grid=(1,),
        out_shape=jax.ShapeDtypeStruct((SEG, 4 * HD), BF16),
        in_specs=[
            pl.BlockSpec(memory_space=pltpu.SMEM),
            row_block,
            pl.BlockSpec((SEG, 4 * HD), lambda i: (0, 0)),
            pl.BlockSpec((HD + 8, HD), lambda i: (0, 0)),
        ],
        out_specs=pl.BlockSpec((SEG, 4 * HD), lambda i: (0, 0)),
        cost_estimate=pl.CostEstimate(flops=48 * SEG * HD * HD, bytes_accessed=2 << 20, transcendentals=4 * SEG * HD),
        compiler_params=pltpu.CompilerParams(vmem_limit_bytes=16 << 20),
        name="mix",
    )(gate, queries, local, memory)


def out_kernel(count, order, *refs):
    mixed_refs, (w_hbm, out_ref, rest_ref, weights, sems) = refs[: 2 * count], refs[2 * count :]
    copies = []
    for p in range(count + 2):
        target = weights.at[p] if p < count else rest_ref.at[p - count]
        mine = [
            pltpu.make_async_copy(
                w_hbm.at[order[p], order[count + 2 + j]], target.at[:, j * HD : (j + 1) * HD], sems.at[p, j]
            )
            for j in range(NY)
        ]
        for copy in mine:
            copy.start()
        copies.append(mine)
    totals = [None, None]
    for p in range(count):
        for copy in copies[p]:
            copy.wait()
        for s in range(2):
            term = jnp.dot(mixed_refs[2 * p + s][...], weights[p], preferred_element_type=F32)
            totals[s] = term if totals[s] is None else totals[s] + term
    for s in range(2):
        out_ref[s * SEG : (s + 1) * SEG, :] = totals[s]
    for mine in copies[count:]:
        for copy in mine:
            copy.wait()


def out_call(order, pieces, weight):
    count = len(pieces)
    vmem = pl.BlockSpec(memory_space=pltpu.VMEM)
    return pl.pallas_call(
        functools.partial(out_kernel, count),
        out_shape=[
            jax.ShapeDtypeStruct((2 * SEG, 4 * HD), F32),
            jax.ShapeDtypeStruct((2, 4 * HD, 4 * HD), BF16),
        ],
        in_specs=[
            pl.BlockSpec(memory_space=pltpu.SMEM),
            *[vmem] * (2 * count),
            pl.BlockSpec(memory_space=pltpu.HBM),
        ],
        out_specs=[vmem, vmem],
        scratch_shapes=[
            pltpu.VMEM((count, 4 * HD, 4 * HD), BF16),
            pltpu.SemaphoreType.DMA((count + 2, NY)),
        ],
        cost_estimate=pl.CostEstimate(flops=4 * count * SEG * 16 * HD * HD, bytes_accessed=(2 * count + 4) << 20, transcendentals=0),
        compiler_params=pltpu.CompilerParams(vmem_limit_bytes=VMEM_LIMIT),
        name="out",
    )(order, *[part for piece in pieces for part in piece], weight)


def add_kernel(which, mixed_0, mixed_1, w_ref, so_far, out_ref):
    for s, mixed_ref in enumerate((mixed_0, mixed_1)):
        at = slice(s * SEG, (s + 1) * SEG)
        term = jnp.dot(mixed_ref[...], w_ref[which], preferred_element_type=F32)
        out_ref[at, :] = (so_far[at, :] + term).astype(out_ref.dtype)


def add_call(which, piece, weights, so_far, dtype):
    vmem = pl.BlockSpec(memory_space=pltpu.VMEM)
    return pl.pallas_call(
        functools.partial(add_kernel, which),
        out_shape=jax.ShapeDtypeStruct(so_far.shape, dtype),
        in_specs=[vmem] * 4,
        out_specs=vmem,
        cost_estimate=pl.CostEstimate(flops=4 * SEG * 16 * HD * HD, bytes_accessed=4 << 20, transcendentals=0),
        compiler_params=pltpu.CompilerParams(vmem_limit_bytes=VMEM_LIMIT),
        name="add",
    )(*piece, weights, so_far)


def per_device(tokens, norm_gain, wq, wk, wv, wo, gate_bias, mem_init, norm_init):
    seq, head = lax.axis_index("seq"), lax.axis_index("head")
    y, z = seq // NZ, seq % NZ
    x, core = head // 2, head % 2

    together = lax.optimization_barrier
    z_index, e_index = jnp.arange(SEQ) // NY, jnp.arange(SEQ) % NY
    order = ((y - e_index) % NY * NZ + z_index).astype(jnp.int32)

    wkv = jnp.concatenate([wk, wv], axis=1)
    wq_1, wq_2, wq_3 = y_move(wq, 1), y_move(wq, 2), y_move(wq, -1)
    one, back = z_move(wkv, 1), z_move(wkv, -1)
    wq_1, wq_2, wq_3, one, back = together((wq_1, wq_2, wq_3, one, back))
    wq_y = jnp.stack([wq, wq_1, wq_2, wq_3])
    trio = jnp.stack([back, wkv, one])
    wkv_p, wkv_m = z_move(trio, 3), z_move(trio[1:], -3)
    wq_y, wkv_p, wkv_m = together((wq_y, wkv_p, wkv_m))
    wq_gathered = z_gather(wq_y)
    wkv_z = jnp.concatenate(
        [wkv[None], back[None], wkv_m[1:], wkv_m[:1], wkv_p[2:], wkv_p[1:2], wkv_p[:1], one[None]]
    )
    wkv_z = lax.dynamic_slice_in_dim(jnp.concatenate([wkv_z, wkv_z[:-1]]), (NZ - z) % NZ, NZ)
    wkv_z, wo = together((wkv_z, wo))
    packs = [wkv_z, y_move(wkv_z, 1), y_move(wkv_z, 2), y_move(wkv_z, -1)]
    wo_own = spread_wo(wo)
    normed = norm_call(tokens, norm_gain, order)
    *packs, normed, wo_own = together((*packs, normed, wo_own))
    wo_y = [wo_own, y_move(wo_own, 1), y_move(wo_own, 2), y_move(wo_own, -1)]
    keys, values, delta = kv_call(normed, packs)
    delta, *wo_y = together((delta, *wo_y))
    wo_y = jnp.stack(wo_y)
    wo_gathered = z_gather(wo_y)

    total = delta[0] + delta[1]
    before = jnp.concatenate([mem_init[0], jnp.broadcast_to(norm_init, (8, HD))], axis=0)
    for bit in (1, 2, 4):
        other = z_swap(total.astype(BF16), bit).astype(F32)
        before = before + jnp.where((z & bit) > 0, other, 0.0)
        total = total + other
    total, wq_gathered = together((total, wq_gathered))
    queries = q_call(normed, wq_gathered.reshape(SEQ, HD, 4 * HD))
    narrow = total.astype(BF16)
    for e, other in ((1, y_move(narrow, 1)), (2, y_move(narrow, 2)), (3, y_move(narrow, -1))):
        before = before + jnp.where(y >= e, other.astype(F32), 0.0)

    gate = jax.nn.sigmoid(gate_bias)
    local = [local_call(queries, keys, values, segment) for segment in range(2)]
    own = [
        mix_call(gate, queries, local[0], before, 0),
        mix_call(gate, queries, local[1], before + delta[0], 1),
    ]

    left = [x_move(own[0], 1)]
    right = [x_move(own[0], -1)]
    left.append(x_move(own[1], 1))
    right.append(x_move(own[1], -1))
    opposite = [x_move(left[0], 1), x_move(right[1], -1)]
    own_swapped = [core_swap(part) for part in own]

    def both(piece):
        return [piece, [core_swap(part) for part in piece]]

    def rows_of(distance):
        index = (x - distance) % NX * 2
        return [index + core, index + 1 - core]

    blocks = [(y - j) % NY for j in range(NY)]
    at = jnp.stack([row for d in (0, 1, -1, 2) for row in rows_of(d)] + blocks).astype(jnp.int32)
    near = [own, own_swapped, *both(left), *both(right)]
    so_far, rest = out_call(at, near, wo_gathered)
    opposite[0], opposite[1], so_far = together((opposite[0], opposite[1], so_far))
    swapped = [core_swap(part) for part in opposite]
    so_far = add_call(0, opposite, rest, so_far, F32)
    swapped[0], swapped[1], so_far = together((swapped[0], swapped[1], so_far))
    return add_call(1, swapped, rest, so_far, BF16)


def solution(mesh):
    placed = (
        P("seq", None),
        P(),
        P("seq", "head"),
        P("seq", "head"),
        P("seq", "head"),
        P("head", "seq"),
        P("head"),
        P("head", None, None),
        P("head", None),
    )
    return jax.shard_map(
        per_device, mesh=mesh, in_specs=placed, out_specs=P("seq", "head"), check_vma=False
    )
```

```python
import functools
import math

import jax
import jax.numpy as jnp
from jax import lax
from jax.experimental import pallas as pl
from jax.experimental.pallas import tpu as pltpu
from jax.sharding import PartitionSpec as P

HD = 128
SEG = 512
NY, NZ, NX = 4, 8, 4
SEQ = NY * NZ
HEADS = 2 * NX
F32 = jnp.float32
BF16 = jnp.bfloat16
VMEM_LIMIT = 20 << 20
VMEM_MOST = 32 << 20


def z_move(block, distance):
    return lax.ppermute(
        block, "seq", [(y * NZ + z, y * NZ + (z + distance) % NZ) for y in range(NY) for z in range(NZ)]
    )


def z_swap(block, bit):
    return lax.ppermute(block, "seq", [(s, s ^ bit) for s in range(SEQ)])


def y_move(block, distance):
    return lax.ppermute(
        block, "seq", [(y * NZ + z, (y + distance) % NY * NZ + z) for y in range(NY) for z in range(NZ)]
    )


def z_gather(block):
    return lax.all_gather(block, "seq", axis=0, axis_index_groups=[[y * NZ + z for z in range(NZ)] for y in range(NY)])


def x_move(block, distance):
    return lax.ppermute(
        block, "head", [(2 * x + c, 2 * ((x + distance) % NX) + c) for x in range(NX) for c in range(2)]
    )


def core_swap(block):
    return lax.ppermute(block, "head", [(h, h ^ 1) for h in range(HEADS)])


def spread_wo(block):
    pairs = []
    for y in range(NY):
        for z in range(NZ):
            for h in range(HEADS):
                pairs.append(((4 * h + y) * HEADS + z, (y * NZ + z) * HEADS + h))
    return lax.ppermute(block, ("seq", "head"), pairs)


def feature_map(values_in):
    return jnp.where(values_in > 0, values_in + 1.0, jnp.exp(jnp.minimum(values_in, 0.0)))


def split(wide):
    high = wide.astype(BF16)
    return high, (wide - high.astype(F32)).astype(BF16)


def norm_kernel(order, x_ref, gain_ref, out_ref):
    wide = x_ref[...].astype(F32)
    scale = lax.rsqrt(jnp.mean(wide * wide, axis=-1, keepdims=True) + 1e-05)
    for block in range(SEQ):
        at = pl.ds(pl.multiple_of(order[block] * HD, HD), HD)
        part = x_ref[:, at].astype(F32) * scale * gain_ref[:, at]
        out_ref[:, block * HD : (block + 1) * HD] = part.astype(BF16)


def norm_call(tokens, gain, order):
    rows, width = tokens.shape
    tile = 128
    return pl.pallas_call(
        norm_kernel,
        out_shape=jax.ShapeDtypeStruct((rows, width), BF16),
        grid_spec=pltpu.PrefetchScalarGridSpec(
            num_scalar_prefetch=1,
            grid=(rows // tile,),
            in_specs=[
                pl.BlockSpec((tile, width), lambda i, o: (i, 0)),
                pl.BlockSpec((1, width), lambda i, o: (0, 0)),
            ],
            out_specs=pl.BlockSpec((tile, width), lambda i, o: (i, 0)),
        ),
        cost_estimate=pl.CostEstimate(flops=6 * rows * width, bytes_accessed=4 * rows * width, transcendentals=rows),
        name="norm",
    )(order, tokens, gain.reshape(1, width))


def fetch(sources, targets, sems):
    copies = [pltpu.make_async_copy(s, t, sems.at[n]) for n, (s, t) in enumerate(zip(sources, targets))]

    @pl.when(pl.program_id(0) == 0)
    def _():
        for copy in copies:
            copy.start()

    return copies


def arrived(copy):
    @pl.when(pl.program_id(0) == 0)
    def _():
        copy.wait()


COLUMNS = 4


def column_blocks(tile, width):
    return [pl.BlockSpec((tile, width // COLUMNS), lambda i, n=n: (i, n)) for n in range(COLUMNS)]


def q_kernel(*refs):
    x_refs, (w_ref, q_ref, held, sems) = refs[:COLUMNS], refs[COLUMNS:]
    size = SEQ // COLUMNS
    parts = [pl.ds(n * size, size) for n in range(COLUMNS)]
    copies = fetch([w_ref.at[part] for part in parts], [held.at[part] for part in parts], sems)
    wide = None
    for n, (copy, x_ref) in enumerate(zip(copies, x_refs)):
        arrived(copy)
        weight = held[n * size : (n + 1) * size].reshape(size * HD, 4 * HD)
        term = jnp.dot(x_ref[...], weight, preferred_element_type=F32)
        wide = term if wide is None else wide + term
    q_ref[...] = wide.astype(BF16)


def q_call(normed, weight):
    rows, width = normed.shape
    tile = 256
    return pl.pallas_call(
        q_kernel,
        grid=(rows // tile,),
        out_shape=jax.ShapeDtypeStruct((rows, 4 * HD), BF16),
        in_specs=[*column_blocks(tile, width), pl.BlockSpec(memory_space=pltpu.HBM)],
        out_specs=pl.BlockSpec((tile, 4 * HD), lambda i: (i, 0)),
        scratch_shapes=[pltpu.VMEM((SEQ, HD, 4 * HD), BF16), pltpu.SemaphoreType.DMA((COLUMNS,))],
        cost_estimate=pl.CostEstimate(flops=2 * rows * width * 4 * HD, bytes_accessed=12 << 20, transcendentals=0),
        compiler_params=pltpu.CompilerParams(vmem_limit_bytes=56 << 20),
        name="q",
    )(*[normed] * COLUMNS, weight)


def kv_kernel(*refs):
    x_refs, pieces = refs[:COLUMNS], refs[COLUMNS : COLUMNS + NY]
    k_ref, v_ref, delta_ref, held, sems = refs[COLUMNS + NY :]
    copies = fetch(pieces, [held.at[:, e] for e in range(NY)], sems)
    for copy in copies:
        arrived(copy)
    each = NZ // COLUMNS
    wide = None
    for n, x_ref in enumerate(x_refs):
        weight = held[n * each : (n + 1) * each].reshape(each * NY * HD, 2 * HD)
        term = jnp.dot(x_ref[...], weight, preferred_element_type=F32)
        wide = term if wide is None else wide + term
    keys = wide[:, :HD].astype(BF16)
    values = wide[:, HD:].astype(BF16)
    k_ref[...] = keys
    v_ref[...] = values
    feats = feature_map(keys.astype(F32))
    high, low = split(feats)
    by_rows = (((0,), (0,)), ((), ()))
    memory = lax.dot_general(high, values, by_rows, preferred_element_type=F32)
    memory += lax.dot_general(low, values, by_rows, preferred_element_type=F32)
    norm = jnp.broadcast_to(jnp.sum(feats, axis=0, keepdims=True), (8, HD))

    @pl.when(pl.program_id(0) % 2 == 0)
    def _():
        delta_ref[0, :HD, :] = memory
        delta_ref[0, HD:, :] = norm

    @pl.when(pl.program_id(0) % 2 == 1)
    def _():
        delta_ref[0, :HD, :] += memory
        delta_ref[0, HD:, :] += norm


def kv_call(normed, pieces):
    rows, width = normed.shape
    tile = SEG // 2
    row_block = pl.BlockSpec((tile, HD), lambda i: (i, 0))
    return pl.pallas_call(
        kv_kernel,
        grid=(rows // tile,),
        out_shape=[
            jax.ShapeDtypeStruct((rows, HD), BF16),
            jax.ShapeDtypeStruct((rows, HD), BF16),
            jax.ShapeDtypeStruct((rows // SEG, HD + 8, HD), F32),
        ],
        in_specs=[*column_blocks(tile, width), *[pl.BlockSpec(memory_space=pltpu.HBM)] * len(pieces)],
        out_specs=[row_block, row_block, pl.BlockSpec((1, HD + 8, HD), lambda i: (i // 2, 0, 0))],
        scratch_shapes=[pltpu.VMEM((NZ, NY, HD, 2 * HD), BF16), pltpu.SemaphoreType.DMA((NY,))],
        cost_estimate=pl.CostEstimate(flops=2 * rows * width * 2 * HD, bytes_accessed=10 << 20, transcendentals=rows * HD),
        compiler_params=pltpu.CompilerParams(vmem_limit_bytes=VMEM_MOST),
        name="kv",
    )(*[normed] * COLUMNS, *pieces)


def local_kernel(q_ref, k_ref, v_ref, out_ref):
    scale = 1.0 / math.sqrt(HD)
    half = SEG // 2
    transposed = (((1,), (1,)), ((), ()))
    for head in range(4):
        for part in range(2):
            rows = slice(part * half, (part + 1) * half)
            seen = (part + 1) * half
            query = q_ref[rows, head * HD : (head + 1) * HD]
            scores = lax.dot_general(query, k_ref[:seen, :], transposed, preferred_element_type=F32) * scale
            row = lax.broadcasted_iota(jnp.int32, (half, seen), 0) + part * half
            column = lax.broadcasted_iota(jnp.int32, (half, seen), 1)
            scores = jnp.where(row >= column, scores, -1e30)
            expd = jnp.exp(scores - jnp.max(scores, axis=-1, keepdims=True))
            probs = (expd / jnp.sum(expd, axis=-1, keepdims=True)).astype(BF16)
            out_ref[rows, head * HD : (head + 1) * HD] = jnp.dot(
                probs, v_ref[:seen, :], preferred_element_type=F32
            )


def local_call(queries, keys, values, segment):
    row_block = lambda n: pl.BlockSpec((SEG, n), lambda i: (segment, 0))
    return pl.pallas_call(
        local_kernel,
        grid=(1,),
        out_shape=jax.ShapeDtypeStruct((SEG, 4 * HD), F32),
        in_specs=[row_block(4 * HD), row_block(HD), row_block(HD)],
        out_specs=pl.BlockSpec((SEG, 4 * HD), lambda i: (0, 0)),
        cost_estimate=pl.CostEstimate(flops=16 * SEG * SEG * HD, bytes_accessed=2 << 20, transcendentals=4 * SEG * SEG),
        compiler_params=pltpu.CompilerParams(vmem_limit_bytes=VMEM_LIMIT),
        name="local",
    )(queries, keys, values)


def mix_kernel(gate_ref, q_ref, local_ref, memory_ref, out_ref):
    memory = memory_ref[:HD, :]
    normer = jnp.broadcast_to(memory_ref[HD : HD + 1, :], (HD, HD)).T
    both_high, both_low = split(jnp.concatenate([memory, normer], axis=1))
    for head in range(4):
        at = slice(head * HD, (head + 1) * HD)
        high, low = split(feature_map(q_ref[:, at].astype(F32)))
        both = jnp.dot(high, both_high, preferred_element_type=F32)
        both += jnp.dot(high, both_low, preferred_element_type=F32)
        both += jnp.dot(low, both_high, preferred_element_type=F32)
        gate = gate_ref[head]
        mixed = gate * (both[:, :HD] / both[:, HD:]) + (1.0 - gate) * local_ref[:, at]
        out_ref[:, at] = mixed.astype(BF16)


def mix_call(gate, queries, local, memory, segment):
    row_block = pl.BlockSpec((SEG, 4 * HD), lambda i: (segment, 0))
    return pl.pallas_call(
        mix_kernel,
        grid=(1,),
        out_shape=jax.ShapeDtypeStruct((SEG, 4 * HD), BF16),
        in_specs=[
            pl.BlockSpec(memory_space=pltpu.SMEM),
            row_block,
            pl.BlockSpec((SEG, 4 * HD), lambda i: (0, 0)),
            pl.BlockSpec((HD + 8, HD), lambda i: (0, 0)),
        ],
        out_specs=pl.BlockSpec((SEG, 4 * HD), lambda i: (0, 0)),
        cost_estimate=pl.CostEstimate(flops=48 * SEG * HD * HD, bytes_accessed=2 << 20, transcendentals=4 * SEG * HD),
        compiler_params=pltpu.CompilerParams(vmem_limit_bytes=16 << 20),
        name="mix",
    )(gate, queries, local, memory)


def out_kernel(count, order, *refs):
    mixed_refs, (w_hbm, out_ref, rest_ref, weights, mixed, sems, mixed_sems) = refs[: 2 * count], refs[2 * count :]
    copies = []
    for p in range(count + 2):
        target = weights.at[p] if p < count else rest_ref.at[p - count]
        mine = [
            pltpu.make_async_copy(
                w_hbm.at[order[p], order[count + 2 + j]], target.at[:, j * HD : (j + 1) * HD], sems.at[p, j]
            )
            for j in range(NY)
        ]
        if p < count:
            mine += [
                pltpu.make_async_copy(mixed_refs[n], mixed.at[n], mixed_sems.at[n]) for n in (2 * p, 2 * p + 1)
            ]
        for copy in mine:
            copy.start()
        copies.append(mine)
    totals = [None, None]
    for p in range(count):
        for copy in copies[p]:
            copy.wait()
        for s in range(2):
            term = jnp.dot(mixed[2 * p + s], weights[p], preferred_element_type=F32)
            totals[s] = term if totals[s] is None else totals[s] + term
    for s in range(2):
        out_ref[s * SEG : (s + 1) * SEG, :] = totals[s]
    for mine in copies[count:]:
        for copy in mine:
            copy.wait()


def out_call(order, pieces, weight):
    count = len(pieces)
    vmem = pl.BlockSpec(memory_space=pltpu.VMEM)
    return pl.pallas_call(
        functools.partial(out_kernel, count),
        out_shape=[
            jax.ShapeDtypeStruct((2 * SEG, 4 * HD), F32),
            jax.ShapeDtypeStruct((2, 4 * HD, 4 * HD), BF16),
        ],
        in_specs=[
            pl.BlockSpec(memory_space=pltpu.SMEM),
            *[pl.BlockSpec(memory_space=pl.ANY)] * (2 * count),
            pl.BlockSpec(memory_space=pltpu.HBM),
        ],
        out_specs=[vmem, vmem],
        scratch_shapes=[
            pltpu.VMEM((count, 4 * HD, 4 * HD), BF16),
            pltpu.VMEM((2 * count, SEG, 4 * HD), BF16),
            pltpu.SemaphoreType.DMA((count + 2, NY)),
            pltpu.SemaphoreType.DMA((2 * count,)),
        ],
        cost_estimate=pl.CostEstimate(flops=4 * count * SEG * 16 * HD * HD, bytes_accessed=(2 * count + 4) << 20, transcendentals=0),
        compiler_params=pltpu.CompilerParams(vmem_limit_bytes=57 << 20),
        name="out",
    )(order, *[part for piece in pieces for part in piece], weight)


def add_kernel(which, mixed_0, mixed_1, w_ref, so_far, out_ref):
    for s, mixed_ref in enumerate((mixed_0, mixed_1)):
        at = slice(s * SEG, (s + 1) * SEG)
        term = jnp.dot(mixed_ref[...], w_ref[which], preferred_element_type=F32)
        out_ref[at, :] = (so_far[at, :] + term).astype(out_ref.dtype)


def add_call(which, piece, weights, so_far, dtype):
    vmem = pl.BlockSpec(memory_space=pltpu.VMEM)
    return pl.pallas_call(
        functools.partial(add_kernel, which),
        out_shape=jax.ShapeDtypeStruct(so_far.shape, dtype),
        in_specs=[vmem] * 4,
        out_specs=vmem,
        cost_estimate=pl.CostEstimate(flops=4 * SEG * 16 * HD * HD, bytes_accessed=4 << 20, transcendentals=0),
        compiler_params=pltpu.CompilerParams(vmem_limit_bytes=VMEM_LIMIT),
        name="add",
    )(*piece, weights, so_far)


def per_device(tokens, norm_gain, wq, wk, wv, wo, gate_bias, mem_init, norm_init):
    seq, head = lax.axis_index("seq"), lax.axis_index("head")
    y, z = seq // NZ, seq % NZ
    x, core = head // 2, head % 2

    together = lax.optimization_barrier
    z_index, e_index = jnp.arange(SEQ) // NY, jnp.arange(SEQ) % NY
    order = ((y - e_index) % NY * NZ + z_index).astype(jnp.int32)

    wkv = jnp.concatenate([wk, wv], axis=1)
    wq_1, wq_2, wq_3 = y_move(wq, 1), y_move(wq, 2), y_move(wq, -1)
    one, back = z_move(wkv, 1), z_move(wkv, -1)
    wq_1, wq_2, wq_3, one, back = together((wq_1, wq_2, wq_3, one, back))
    wq_y = jnp.stack([wq, wq_1, wq_2, wq_3])
    trio = jnp.stack([back, wkv, one])
    wkv_p, wkv_m = z_move(trio, 3), z_move(trio[1:], -3)
    wq_y, wkv_p, wkv_m = together((wq_y, wkv_p, wkv_m))
    wq_gathered = z_gather(wq_y)
    wkv_z = jnp.concatenate(
        [wkv[None], back[None], wkv_m[1:], wkv_m[:1], wkv_p[2:], wkv_p[1:2], wkv_p[:1], one[None]]
    )
    wkv_z = lax.dynamic_slice_in_dim(jnp.concatenate([wkv_z, wkv_z[:-1]]), (NZ - z) % NZ, NZ)
    wkv_z, wo = together((wkv_z, wo))
    packs = [wkv_z, y_move(wkv_z, 1), y_move(wkv_z, 2), y_move(wkv_z, -1)]
    wo_own = spread_wo(wo)
    normed = norm_call(tokens, norm_gain, order)
    *packs, normed, wo_own = together((*packs, normed, wo_own))
    wo_y = [wo_own, y_move(wo_own, 1), y_move(wo_own, 2), y_move(wo_own, -1)]
    keys, values, delta = kv_call(normed, packs)
    delta, *wo_y = together((delta, *wo_y))
    wo_y = jnp.stack(wo_y)
    wo_gathered = z_gather(wo_y)

    total = delta[0] + delta[1]
    before = jnp.concatenate([mem_init[0], jnp.broadcast_to(norm_init, (8, HD))], axis=0)
    for bit in (1, 2, 4):
        other = z_swap(total.astype(BF16), bit).astype(F32)
        before = before + jnp.where((z & bit) > 0, other, 0.0)
        total = total + other
    total, wq_gathered = together((total, wq_gathered))
    queries = q_call(normed, wq_gathered.reshape(SEQ, HD, 4 * HD))
    narrow = total.astype(BF16)
    for e, other in ((1, y_move(narrow, 1)), (2, y_move(narrow, 2)), (3, y_move(narrow, -1))):
        before = before + jnp.where(y >= e, other.astype(F32), 0.0)

    gate = jax.nn.sigmoid(gate_bias)
    local = [local_call(queries, keys, values, segment) for segment in range(2)]
    own = [
        mix_call(gate, queries, local[0], before, 0),
        mix_call(gate, queries, local[1], before + delta[0], 1),
    ]

    left = [x_move(own[0], 1)]
    right = [x_move(own[0], -1)]
    left.append(x_move(own[1], 1))
    right.append(x_move(own[1], -1))
    opposite = [x_move(left[0], 1), x_move(right[1], -1)]
    own_swapped = [core_swap(part) for part in own]

    def both(piece):
        return [piece, [core_swap(part) for part in piece]]

    def rows_of(distance):
        index = (x - distance) % NX * 2
        return [index + core, index + 1 - core]

    blocks = [(y - j) % NY for j in range(NY)]
    at = jnp.stack([row for d in (0, 1, -1, 2) for row in rows_of(d)] + blocks).astype(jnp.int32)
    near = [own, own_swapped, *both(left), *both(right)]
    so_far, rest = out_call(at, near, wo_gathered)
    opposite[0], opposite[1], so_far = together((opposite[0], opposite[1], so_far))
    swapped = [core_swap(part) for part in opposite]
    so_far = add_call(0, opposite, rest, so_far, F32)
    swapped[0], swapped[1], so_far = together((swapped[0], swapped[1], so_far))
    return add_call(1, swapped, rest, so_far, BF16)


def solution(mesh):
    placed = (
        P("seq", None),
        P(),
        P("seq", "head"),
        P("seq", "head"),
        P("seq", "head"),
        P("head", "seq"),
        P("head"),
        P("head", None, None),
        P("head", None),
    )
    return jax.shard_map(
        per_device, mesh=mesh, in_specs=placed, out_specs=P("seq", "head"), check_vma=False
    )
```
